32 devices in a mesh: shard: 8 (over z, y), tensor: 4 (over x, core).
Axes of the slice: x: 2, y: 2, z: 4, core: 2. Of those that a mesh axis runs over, the one named last changes fastest.
Arguments:
- acts: bfloat16 [2048, 1152], P('shard', 'tensor'), may hold values from -600 to 600
- outgrads: bfloat16 [2048, 1152], P('shard', 'tensor'), may hold values from -800 to 800
- weight: bfloat16 [1152, 1152], P('shard', 'tensor'), may hold values from -6 to 6
- momentum: float32 [1152, 1152], P('shard', 'tensor'), may hold values from -6 to 6
- damping: float32 [2], replicated, may hold values from 0.3 to 3
- coeffs: float32 [4], replicated, may hold values from 0.5 to 2
Outputs:
- new_momentum: float32 [1152, 1152], P('shard', 'tensor')
- gathered_weight: bfloat16 [1152, 1152], P(None, 'tensor')
The draws below stay inside these ranges and needn't reach their ends.
All inputs are finite; a program needn't handle non-finite values.
Results may differ from the reference program's by a relative error of at most 0.003.
The reference program's roundings to bfloat16 on the way (of `act_factor`, `grad_factor`, `grad_inverse` and `projected`) count: a program that leaves them out, or rounds other values in their place, can miss the bound.
Values may be sent and summed in bfloat16 or wider, within the bound.
A program may use at most 64 MiB of HBM per device.

```python
import math
import jax
import jax.numpy as jnp
from jax import lax

D = 1152
TERMS = 4
TOKENS = 2048


def draw_pair(key):
    base_key = jax.random.fold_in(key, 11)
    keys = jax.random.split(base_key, 4)
    col_pos = jnp.arange(D, dtype=jnp.float32)[None, :] / (D - 1)
    tok_pos = jnp.arange(TOKENS, dtype=jnp.float32)[:, None] / (TOKENS - 1)
    noise_act = jax.random.truncated_normal(keys[0], -4.0, 4.0, (TOKENS, D), jnp.float32)
    noise_grad = jax.random.truncated_normal(keys[1], -4.0, 4.0, (TOKENS, D), jnp.float32)
    col_scale = jnp.power(3.0, col_pos) * jnp.exp(jax.random.uniform(keys[2], (1, D), jnp.float32, 0.0, 1.2))
    row_scale = jnp.power(3.0, tok_pos) * jnp.exp(jax.random.uniform(keys[3], (TOKENS, 1), jnp.float32, 0.0, 1.0))
    mixed = noise_act + 0.5 * jnp.roll(noise_act, 1, axis=1)
    acts_value = mixed * col_scale * row_scale
    grad_mixed = 0.6 * jnp.roll(mixed, 5, axis=1) + noise_grad + 0.4 * jnp.roll(noise_grad, 3, axis=1)
    grads_value = grad_mixed * jnp.roll(col_scale, 5, axis=1) * row_scale
    return (acts_value, grads_value)


def draw_acts(key, part):
    return draw_pair(key)[0].astype(jnp.bfloat16)


def draw_outgrads(key, part):
    return draw_pair(key)[1].astype(jnp.bfloat16)


def steps_of(stream_key, shape, cuts, smallest, high):
    def one(dim, parts):
        heights = jax.random.uniform(jax.random.fold_in(jax.random.fold_in(stream_key, 6), dim), (parts,), jnp.float32, smallest / len(cuts), high / len(cuts))
        return jnp.repeat(jnp.exp(heights), shape[dim] // parts).reshape((-1,) + (1,) * (len(shape) - dim - 1))

    gain = one(*cuts[0])
    for cut in cuts[1:]:
        gain = gain * one(*cut)
    return gain


def centred(key, shape, width, reach, cuts=(), held_as=jnp.bfloat16):
    array = jax.random.normal(key, shape, jnp.float32) * width
    if len(cuts) > 0:
        array = steps_of(key, shape, cuts, -0.22, 0.18) * array
    return jnp.clip(array, min=-reach, max=reach).astype(held_as)


def setup_inputs(seed: int = 0) -> dict:
    key_of = jax.random.split(jax.random.key(seed), 7)
    acts = draw_acts(jax.random.fold_in(key_of[6], 71), 0)
    outgrads = draw_outgrads(jax.random.fold_in(key_of[6], 71), 0)
    weight = centred(key_of[2], (D, D), 1.0, 6.0, ((0, 8), (1, 4)))
    momentum = centred(key_of[3], (D, D), 1.0, 6.0, ((0, 8), (1, 4)), jnp.float32)
    damping = jnp.clip(jnp.exp(jax.random.uniform(key_of[4], (2,), jnp.float32, math.log(0.3), math.log(3.0))), 0.3, 3.0)
    coeffs = jnp.clip(jnp.exp(jax.random.uniform(key_of[5], (TERMS,), jnp.float32, math.log(0.5), math.log(2.0))), 0.5, 2.0)
    return {"acts": acts, "outgrads": outgrads, "weight": weight, "momentum": momentum, "damping": damping, "coeffs": coeffs}


def horner_columns(factor, coeffs, first_col, col_count, bound_norm):
    extent = factor.shape[0]
    row_ids = lax.broadcasted_iota(jnp.int32, (extent, col_count), 0)
    col_ids = lax.broadcasted_iota(jnp.int32, (extent, col_count), 1) + first_col
    identity_cols = (row_ids == col_ids).astype(jnp.float32)
    term_count = coeffs.shape[0]
    iterate = coeffs[term_count - 1] * identity_cols
    for term_index in range(term_count - 2, -1, -1):
        product = jnp.dot(factor, iterate.astype(jnp.bfloat16), preferred_element_type=jnp.float32)
        iterate = coeffs[term_index] * identity_cols + iterate - product / bound_norm
    return iterate

def reference(acts, outgrads, weight, momentum, damping, coeffs):
    act_cov = jnp.dot(acts.T, acts, preferred_element_type=jnp.float32)
    grad_cov = jnp.dot(outgrads.T, outgrads, preferred_element_type=jnp.float32)
    act_trace = jnp.sum(jnp.square(acts.astype(jnp.float32)))
    grad_trace = jnp.sum(jnp.square(outgrads.astype(jnp.float32)))
    identity = jnp.eye(D, dtype=jnp.float32)
    act_factor = (act_cov + damping[0] * act_trace / D * identity).astype(jnp.bfloat16)
    grad_factor = (grad_cov + damping[1] * grad_trace / D * identity).astype(jnp.bfloat16)
    act_scale = jnp.sqrt(jnp.sum(jnp.square(act_factor.astype(jnp.float32))))
    grad_scale = jnp.sqrt(jnp.sum(jnp.square(grad_factor.astype(jnp.float32))))
    act_inverse = horner_columns(act_factor, coeffs, 0, D, act_scale)
    grad_inverse = horner_columns(grad_factor, coeffs, 0, D, grad_scale).astype(jnp.bfloat16)
    projected = jnp.dot(outgrads, grad_inverse, preferred_element_type=jnp.float32).astype(jnp.bfloat16)
    right_product = jnp.dot(acts.T, projected, preferred_element_type=jnp.float32)
    update = jnp.dot(act_inverse.T, right_product, precision=lax.Precision.HIGHEST)
    mean_square = jnp.sum(update * update) / (D * D)
    new_momentum = 0.9 * momentum + update / jnp.sqrt(mean_square + 1e-06)
    gathered_weight = (weight.astype(jnp.float32) - 0.1 * new_momentum).astype(jnp.bfloat16)
    return (new_momentum, gathered_weight)
```

```python
import functools

import jax
import jax.numpy as jnp
from jax import lax
from jax.experimental import pallas as pl
from jax.experimental.pallas import tpu as pltpu
from jax.sharding import PartitionSpec as P

D = 1152


def horner_columns(factor, coeffs, first_col, col_count, bound_norm):
    extent = factor.shape[0]
    row_ids = lax.broadcasted_iota(jnp.int32, (extent, col_count), 0)
    col_ids = lax.broadcasted_iota(jnp.int32, (extent, col_count), 1) + first_col
    identity_cols = (row_ids == col_ids).astype(jnp.float32)
    term_count = coeffs.shape[0]
    iterate = coeffs[term_count - 1] * identity_cols
    for term_index in range(term_count - 2, -1, -1):
        product = jnp.dot(factor, iterate.astype(jnp.bfloat16), preferred_element_type=jnp.float32)
        iterate = coeffs[term_index] * identity_cols + iterate - product / bound_norm
    return iterate


def tokens_product(left, right):
    return lax.dot_general(
        left, right, (((0,), (0,)), ((), ())), preferred_element_type=jnp.float32
    )


def on_device(acts, outgrads, weight, momentum, damping, coeffs):
    row_count = weight.shape[0]
    col_count = weight.shape[1]
    row_first = lax.axis_index("shard") * row_count
    col_first = lax.axis_index("tensor") * col_count
    full_acts, full_grads = (
        lax.all_gather(acts, "tensor", axis=1, tiled=True),
        lax.all_gather(outgrads, "tensor", axis=1, tiled=True),
    )
    local_squares = jnp.stack(
        [
            jnp.sum(jnp.square(acts.astype(jnp.float32))),
            jnp.sum(jnp.square(outgrads.astype(jnp.float32))),
        ]
    )
    traces = lax.psum(local_squares, ("shard", "tensor"))
    act_part = tokens_product(full_acts, acts)
    grad_part = tokens_product(full_grads, outgrads)
    stats = lax.psum_scatter(
        jnp.concatenate([act_part, grad_part], axis=1), "shard", scatter_dimension=0, tiled=True
    )
    row_ids = lax.broadcasted_iota(jnp.int32, (row_count, col_count), 0) + row_first
    col_ids = lax.broadcasted_iota(jnp.int32, (row_count, col_count), 1) + col_first
    diag_mask = (row_ids == col_ids).astype(jnp.float32)
    act_piece = (stats[:, :col_count] + damping[0] * traces[0] / D * diag_mask).astype(jnp.bfloat16)
    grad_piece = (stats[:, col_count:] + damping[1] * traces[1] / D * diag_mask).astype(
        jnp.bfloat16
    )
    act_wide, grad_wide = (
        lax.all_gather(act_piece, "tensor", axis=1, tiled=True),
        lax.all_gather(grad_piece, "tensor", axis=1, tiled=True),
    )
    act_full, grad_full = (
        lax.all_gather(act_wide, "shard", axis=0, tiled=True),
        lax.all_gather(grad_wide, "shard", axis=0, tiled=True),
    )
    act_scale = jnp.sqrt(jnp.sum(jnp.square(act_full.astype(jnp.float32))))
    grad_scale = jnp.sqrt(jnp.sum(jnp.square(grad_full.astype(jnp.float32))))
    act_inverse = horner_columns(act_full, coeffs, row_first, row_count, act_scale)
    grad_inverse = horner_columns(grad_full, coeffs, col_first, col_count, grad_scale).astype(
        jnp.bfloat16
    )
    projected = jnp.dot(full_grads, grad_inverse, preferred_element_type=jnp.float32).astype(
        jnp.bfloat16
    )
    right_term = tokens_product(full_acts, projected)
    right_product = lax.psum(right_term, "shard")
    update = lax.dot_general(
        act_inverse,
        right_product,
        (((0,), (0,)), ((), ())),
        precision=lax.Precision.HIGHEST,
        preferred_element_type=jnp.float32,
    )
    square_sum = lax.psum(jnp.sum(update * update), ("shard", "tensor"))
    mean_square = square_sum / (D * D)
    new_momentum = 0.9 * momentum + update / jnp.sqrt(mean_square + 1e-06)
    new_weight = (weight.astype(jnp.float32) - 0.1 * new_momentum).astype(jnp.bfloat16)
    gathered_weight = lax.all_gather(new_weight, "shard", axis=0, tiled=True)
    return (new_momentum, gathered_weight)


MESH = pl.DeviceIdType.MESH
BF16 = jnp.bfloat16
F32 = jnp.float32
X_CHIPS = 2
Y_CHIPS = 2
CORES = 2
TILES = 3
PLANES = 4
PARTS = 2


def dot_nt(left, right):
    return lax.dot_general(
        left, right, (((1,), (1,)), ((), ())), preferred_element_type=jnp.float32
    )


def dot_nn(left, right, precision=None):
    return lax.dot_general(
        left,
        right,
        (((1,), (0,)), ((), ())),
        precision=precision,
        preferred_element_type=jnp.float32,
    )


def eye(rows, cols, row_first, col_first):
    row_ids = lax.broadcasted_iota(jnp.int32, (rows, cols), 0) + row_first
    col_ids = lax.broadcasted_iota(jnp.int32, (rows, cols), 1) + col_first
    return row_ids == col_ids


def total(value):
    return jnp.sum(jnp.sum(value, axis=0, keepdims=True), axis=1, keepdims=True)


class Place:
    def __init__(self):
        self.s = lax.axis_index("shard")
        self.t = lax.axis_index("tensor")
        self.z, self.y = self.s // Y_CHIPS, self.s % Y_CHIPS
        self.x, self.c = self.t // CORES, self.t % CORES
        z, y, x, c = self.z, self.y, self.x, self.c
        self.mid = ((z + 1) // 2) % 2
        self.own = (y, x)
        self.p = (c * (1 - y) + (1 - c) * y, (1 - c) * (1 - x) + c * x)
        self.q = ((1 - c) * (1 - y) + c * y, c * (1 - x) + (1 - c) * x)
        self.d = (1 - y, 1 - x)

    def id(self, z, chip, c):
        return (z * Y_CHIPS + chip[0], chip[1] * CORES + c)

    def plane(self, k):
        z = self.z
        if isinstance(k, int):
            return [z, z + 1 - 2 * (z % 2), (z + 2) % PLANES, PLANES - 1 - z][k]
        return (k - 2) * (PLANES - 1 - z) + (3 - k) * ((z + 2) % PLANES)

    def slab(self, far, j):
        return self.plane(self.nth(j)) * Y_CHIPS + [self.y, 1 - self.y][far]

    def nth(self, j):
        return [0, 1, 2 + self.mid, 3 - self.mid][j]


class Stream:
    SLOTS = {"L": (8, 4), "P": (4, 4), "Q": (4, 4), "D": (8, 4)}

    def __init__(self, place, buf, width, first, count, sems):
        self.at, self.buf, self.width = place, buf, width
        self.first, self.count, self.sems = first, count, sems

    def block(self, k, chip, c):
        p = self.at
        rows = pl.multiple_of((c * X_CHIPS + chip[1]) * self.width + self.first, 16)
        return self.buf.at[p.plane(k) * Y_CHIPS + chip[0], pl.ds(rows, self.count), :]

    def copy(self, kind, index, ref, target, slot=None):
        send, recv = self.sems[kind]
        return pltpu.make_async_remote_copy(
            src_ref=ref,
            dst_ref=ref,
            send_sem=send.at[index if slot is None else slot],
            recv_sem=recv.at[index],
            device_id=target,
            device_id_type=MESH,
        )

    def arrive(self, kind, index, ref):
        p = self.at
        self.copy(kind, index, ref, p.id(p.z, p.own, 1 - p.c), 0).wait_recv()

    def to_p(self, kind, index, ref):
        p = self.at
        self.copy(kind, index, ref, p.id(p.z, p.p, p.c)).start()

    def to_q(self, kind, index, ref):
        p = self.at
        self.copy(kind, index, ref, p.id(p.z, p.q, p.c)).start()

    def to_plane(self, kind, index, ref, k, slot):
        p = self.at
        self.copy(kind, index, ref, p.id(p.plane(k), p.own, p.c), slot).start()

    def mid_to_plane(self, kind, index, ref, k, slot):
        @pl.when(self.at.mid == 1)
        def _():
            self.to_plane(kind, index, ref, k, slot)

    def own(self):
        p = self.at
        return self.block(0, p.own, p.c)

    def own_across(self):
        self.to_p("P", 0, self.own())
        self.to_q("Q", 0, self.own())

    def own_along(self):
        self.to_plane("L", 1, self.own(), 1, 1)
        self.mid_to_plane("L", 3, self.own(), 3, 3)

    def line(self, j):
        p = self.at
        k = p.nth(j)
        ref = self.block(k, p.own, p.c)
        self.arrive("L", k, ref)
        if j == 1:
            self.mid_to_plane("L", 2, ref, 3, 2)
        elif j == 2:
            self.mid_to_plane("L", 2, ref, 1, 6)
        else:
            self.mid_to_plane("L", 3, ref, 1, 7)
        self.to_p("P", k, ref)
        self.to_q("Q", k, ref)

    def pcol(self, j):
        p = self.at
        k = p.nth(j)
        ref = self.block(k, p.p, p.c)
        self.arrive("P", k, ref)
        if j == 3:
            self.to_q("D", k, ref)

    def qcol(self, j):
        p = self.at
        k = p.nth(j)
        ref = self.block(k, p.q, p.c)
        self.arrive("Q", k, ref)
        if j == 0:
            self.to_p("D", 0, ref)

    def diag(self, j):
        p = self.at
        k = p.nth(j)
        ref = self.block(k, p.d, p.c)
        self.arrive("D", k, ref)
        if j == 0:
            self.to_plane("D", 1, ref, 1, 5)
            self.mid_to_plane("D", 3, ref, 3, 7)
        if j == 2:
            self.mid_to_plane("D", 2, ref, 1, 6)

    def finish(self):
        p = self.at

        def sent(kind, slot):
            self.copy(kind, 0, self.own(), p.id(p.z, p.own, 1 - p.c), slot).wait_send()

        for k in range(4):
            sent("P", k)
            sent("Q", k)
        sent("L", 1)
        sent("D", 0)
        sent("D", 3 - p.mid)
        sent("D", 5)

        @pl.when(p.mid == 1)
        def _():
            for slot in (2, 3, 6, 7):
                sent("L", slot)
            for slot in (6, 7):
                sent("D", slot)


class Sibling:
    def __init__(self, place, buf, sems):
        self.at, self.buf, self.sems = place, buf, sems

    def copy(self, far, j, c):
        p = self.at
        k = p.nth(j)
        half = self.buf.shape[1] // CORES
        rows = pl.multiple_of(c * half, 16)
        ref = self.buf.at[p.slab(far, j), pl.ds(rows, half), :]
        return pltpu.make_async_remote_copy(
            src_ref=ref,
            dst_ref=ref,
            send_sem=self.sems[0].at[PLANES * far + k],
            recv_sem=self.sems[1].at[PLANES * far + k],
            device_id=p.id(p.z, p.own, 1 - p.c),
            device_id_type=MESH,
        )

    def send(self, far, j):
        self.copy(far, j, self.at.c).start()

    def arrive(self, far, j):
        self.copy(far, j, 1 - self.at.c).wait_recv()

    def finish(self):
        for far in range(2):
            for j in range(PLANES):
                self.copy(far, j, self.at.c).wait_send()


def cov_slab(buf, cov, slab, add):
    tile = cov.shape[0] // TILES
    for i in range(TILES):
        for j in range(i, TILES):
            rows, cols = pl.ds(i * tile, tile), pl.ds(j * tile, tile)
            product = dot_nt(buf[slab, rows, :], buf[slab, cols, :])
            cov[rows, cols] = cov[rows, cols] + product if add else product


def right_slab(buf, projected, right, slab, add):
    tile = right.shape[0] // TILES
    for i in range(TILES):
        rows = pl.ds(i * tile, tile)
        product = dot_nt(buf[slab, rows, :], projected[slab])
        right[rows, :] = right[rows, :] + product if add else product


def damp(cov, factor, damping):
    d = cov.shape[0]
    step = d // 9
    trace = jnp.zeros((1, 1), F32)
    for i in range(9):
        part = cov[i * step : (i + 1) * step, i * step : (i + 1) * step]
        trace = trace + total(jnp.where(eye(step, step, 0, 0), part, 0.0))
    shift = damping * trace / d

    tile = d // TILES
    unit = eye(tile, tile, 0, 0)
    ones = unit.astype(F32).astype(BF16)
    squares = jnp.zeros((1, tile), F32)
    for i in range(TILES):
        for j in range(i, TILES):
            rows, cols = slice(i * tile, (i + 1) * tile), slice(j * tile, (j + 1) * tile)
            piece = cov[rows, cols]
            if i == j:
                piece = piece + jnp.where(unit, shift, 0.0)
            low = piece.astype(BF16)
            factor[rows, cols] = low
            wide = low.astype(F32)
            square = jnp.sum(wide * wide, axis=0, keepdims=True)
            squares = squares + (square if i == j else 2.0 * square)
            if i != j:
                factor[cols, rows] = dot_nt(ones, low).astype(BF16)
    return jnp.sqrt(jnp.sum(squares, axis=1, keepdims=True))


def horner_steps(factor, work, coeffs, first, norm):
    rows, d = work.shape
    tile = d // TILES
    terms = coeffs.shape[0]

    def begin():
        start = pl.multiple_of(first, rows)
        top = jnp.full((1, 1), coeffs[terms - 1], F32).astype(BF16).astype(F32)
        diag = eye(rows, d, first, 0)
        value = jnp.where(diag, coeffs[terms - 2] + coeffs[terms - 1], 0.0)
        work[...] = value - factor[pl.ds(start, rows), :].astype(F32) * (top / norm())

    def term(index):
        low = work[...].astype(BF16)
        inv = 1.0 / norm()
        for j in range(TILES):
            cols = slice(j * tile, (j + 1) * tile)
            product = dot_nn(low, factor[:, cols])
            held = jnp.where(eye(rows, tile, first, j * tile), coeffs[index], 0.0)
            work[:, cols] = held + work[:, cols] - product * inv

    return [begin] + [functools.partial(term, k) for k in range(terms - 3, -1, -1)]


PLAN = [
    "GX GZ AX AZ",
    "GQ0 GO1 GO2m GP0",
    "GD0 GN0 GF0 GO3m",
    "AP0 GO2e gn0 AQ0",
    "GQ1 AN0 GP1 GO3e",
    "GN1 gf0 an0 GP2",
    "gn1 GD2 GD1 GQ2",
    "GF2 GF1 GN2 GP3",
    "AO1 AO2m GQ3 GN3",
    "gf2 gn2 AD0 AF0",
    "AO2e gn3 GD3 GF3",
    "gf1 af0 AO3m gf3",
    "gd h0 AO3e h1",
    "h2 AQ1 hl AP1",
    "p0 AN1 p1 p2",
    "p3 AD2 AP3 AP2",
    "AQ2 AF2 AN2 rn0",
    "rf0 AD1 an1 AQ3",
    "AN3 AF1 rn1 af2",
    "rf2 an2 rn2 AD3",
    "AF3 an3 af1 rn3",
    "rf1 af3 rf3",
]


def step_kernel(
    acts_ref,
    grads_ref,
    weight_ref,
    momentum_ref,
    damping_ref,
    coeffs_ref,
    new_momentum_ref,
    weights_ref,
    acts_all,
    grads_all,
    cov,
    act_cov,
    factor,
    grad_work,
    grad_low,
    act_work,
    projected,
    right,
    weight_all,
    weight_own,
    momentum,
    sums,
    local_sems,
    sum_send,
    sum_recv,
    *sems,
):
    p = Place()
    s, t = p.s, p.t
    shards, tensors = Y_CHIPS * PLANES, X_CHIPS * CORES
    width = grads_ref.shape[0]
    height, d = weight_ref.shape[0], cov.shape[0]
    barrier = pltpu.get_barrier_semaphore()
    others = []
    for k in range(1, shards * tensors):
        others.append(((s + k // tensors) % shards, (t + k % tensors) % tensors))
    for other in others:
        pl.semaphore_signal(barrier, inc=1, device_id=other, device_id_type=MESH)

    place = p.c * X_CHIPS + p.x
    own_rows = pl.ds(pl.multiple_of(place * width, width), width)
    loads = []
    for k, (src, dst) in enumerate(
        [
            (grads_ref, grads_all.at[s, own_rows, :]),
            (acts_ref, acts_all.at[s, own_rows, :]),
            (weight_ref, weight_own),
            (momentum_ref, momentum),
        ]
    ):
        loads.append(pltpu.make_async_copy(src, dst, local_sems.at[k]))
        loads[-1].start()

    pairs = list(zip(sems[0::2], sems[1::2]))
    kinds = list(Stream.SLOTS)
    part = width // PARTS
    streams, siblings = {}, {}
    for name, buf in (("G", grads_all), ("A", acts_all)):
        streams[name] = []
        for k in range(PARTS):
            own = dict(zip(kinds, pairs[: len(kinds)]))
            pairs = pairs[len(kinds) :]
            streams[name].append(Stream(p, buf, width, k * part, part, own))
        siblings[name] = Sibling(p, buf, pairs[0])
        pairs = pairs[1:]
    line_pair, cross_pair = pairs

    loads[0].wait()
    loads[1].wait()
    pl.semaphore_wait(barrier, len(others))

    def relay(word):
        if word[1] in "NF":
            siblings[word[0]].send("NF".index(word[1]), int(word[2]))
            return
        for stream in streams[word[0]]:
            if word[1] in "XZ":
                {"X": stream.own_across, "Z": stream.own_along}[word[1]]()
            else:
                move = {"O": stream.line, "P": stream.pcol, "Q": stream.qcol, "D": stream.diag}[word[1]]
                move(int(word[2]))

    norms = {}
    horner_g = horner_steps(factor, grad_work, coeffs_ref, place * width, lambda: norms["g"])
    started = set()

    def compute(word):
        kind = word[0]
        if word == "gd":
            norms["g"] = damp(cov, factor, damping_ref[1])
        elif word == "hl":
            grad_low[...] = grad_work[...].astype(BF16)
        elif kind == "h":
            horner_g[int(word[1])]()
        elif kind == "p":
            for k in (2 * int(word[1]), 2 * int(word[1]) + 1):
                projected[k] = dot_nn(grad_low[...], grads_all[k]).astype(BF16)
        else:
            far, j = "nf".index(word[1]), int(word[2])
            slab = p.slab(far, j)
            add = kind in started
            started.add(kind)
            if kind == "r":
                right_slab(acts_all, projected, right, slab, add)
            else:
                name = kind.upper()
                siblings[name].arrive(far, j)
                buf, out = {"G": (grads_all, cov), "A": (acts_all, act_cov)}[name]
                cov_slab(buf, out, slab, add)

    for word in " ".join(PLAN).split():
        if word[0] not in "GA":
            compute(word)
        elif word[-1] in "em":
            @pl.when(p.mid == "em".index(word[-1]))
            def _():
                relay(word[:-1])
        else:
            relay(word)

    act_norm = damp(act_cov, factor, damping_ref[0])
    block, inner = s * height // width, s * height % width
    first = (block % CORES * X_CHIPS + block // CORES) * width + inner
    for run in horner_steps(factor, act_work, coeffs_ref, first, lambda: act_norm):
        run()
    update = dot_nn(act_work[...], right[...], lax.Precision.HIGHEST)

    me = s * tensors + t
    sums[me] = jnp.broadcast_to(total(update * update), sums.shape[1:])
    count = shards * tensors
    for k, other in enumerate(others):
        pltpu.make_async_remote_copy(
            src_ref=sums.at[me],
            dst_ref=sums.at[me],
            send_sem=sum_send,
            recv_sem=sum_recv,
            device_id=other,
            device_id_type=MESH,
        ).start()
    loads[2].wait()
    loads[3].wait()
    for name in streams:
        siblings[name].finish()
        for stream in streams[name]:
            stream.finish()
    everyone = pltpu.make_async_remote_copy(
        src_ref=sums.at[: count - 1],
        dst_ref=sums.at[: count - 1],
        send_sem=sum_send,
        recv_sem=sum_recv,
        device_id=others[0],
        device_id_type=MESH,
    )
    everyone.wait_recv()
    square_sum = jnp.sum(sums[...], axis=0)[:, 0:1]
    mean_square = square_sum / (d * d)
    new = 0.9 * momentum[...] + update / jnp.sqrt(mean_square + 1e-06)
    momentum[...] = new
    low = (weight_own[...].astype(F32) - 0.1 * new).astype(BF16)
    main = weight_all.shape[2]
    rest = width - main
    weight_all[s, :height, :] = low[:, :main]
    ones = eye(rest, rest, 0, 0).astype(F32).astype(BF16)
    weight_all[s, height:, :height] = dot_nt(ones, low[:, main:]).astype(BF16)

    sent = []
    cuts = [slice(0, 96), slice(96, weight_all.shape[1])]

    def push(slab, pair, k, cut, target):
        part = weight_all.at[slab, cuts[cut], :]
        copy = pltpu.make_async_remote_copy(
            src_ref=part,
            dst_ref=part,
            send_sem=pair[0].at[k, cut],
            recv_sem=pair[1].at[k, cut],
            device_id=target,
            device_id_type=MESH,
        )
        copy.start()
        sent.append(copy)
        return copy

    across = (p.z * Y_CHIPS + 1 - p.y, t)
    order = [p.nth(j) for j in range(PLANES - 1, 0, -1)]
    crossed, lines = [], []
    for cut in range(len(cuts)):
        crossed.append((0, push(s, cross_pair, 0, cut, across)))
        for k in order:
            lines.append((k, cut, push(s, line_pair, k, cut, (p.plane(k) * Y_CHIPS + p.y, t))))
    stores = [pltpu.make_async_copy(momentum, new_momentum_ref, local_sems.at[4])]
    stores[0].start()

    def keep(slab):
        stores.append(
            pltpu.make_async_copy(
                weight_all.at[slab], weights_ref.at[slab], local_sems.at[4 + len(stores)]
            )
        )
        stores[-1].start()

    keep(s)
    for k in order:
        slab = p.plane(k) * Y_CHIPS + p.y
        for j, cut, copy in lines:
            if j is k:
                copy.wait_recv()
                crossed.append((k, push(slab, cross_pair, k, cut, across)))
        keep(slab)
    for k in [0] + order:
        for j, copy in crossed:
            if j is k:
                copy.wait_recv()
        keep(p.plane(k) * Y_CHIPS + 1 - p.y)
    for copy in sent:
        copy.wait_send()
    everyone.wait_send()
    for copy in stores:
        copy.wait()


def finish_kernel(momentum_ref, weights_ref, new_momentum_ref, gathered_ref):
    shards, rows, main = weights_ref.shape
    width = gathered_ref.shape[0]
    height = rows - (width - main)
    new_momentum_ref[...] = momentum_ref[...]
    low = jnp.concatenate([weights_ref[k, :height, :] for k in range(shards)], axis=0)
    ones = eye(main, main, 0, 0).astype(F32).astype(BF16)
    gathered_ref[:main, :] = dot_nt(ones, low).astype(BF16)
    for k in range(shards):
        gathered_ref[main:, k * height : (k + 1) * height] = weights_ref[k, height:, :height]


def on_device_whole(acts, outgrads, weight, momentum, damping, coeffs):
    tokens, width = acts.shape
    height = weight.shape[0]
    shards, tensors = Y_CHIPS * PLANES, X_CHIPS * CORES
    d = width * tensors
    main = width // 128 * 128
    packed = (shards, height + width - main, main)
    vmem = pl.BlockSpec(memory_space=pltpu.VMEM)
    smem = pl.BlockSpec(memory_space=pltpu.SMEM)
    anywhere = pl.BlockSpec(memory_space=pl.ANY)
    dma = pltpu.SemaphoreType.DMA
    sems = []
    for _ in range(2):
        for pair in list(Stream.SLOTS.values()) * PARTS + [(CORES * PLANES, CORES * PLANES)]:
            sems += [dma((count,)) for count in pair]
    new_momentum, weights = pl.pallas_call(
        step_kernel,
        out_shape=(
            jax.ShapeDtypeStruct((height, width), F32),
            jax.ShapeDtypeStruct(packed, BF16),
        ),
        in_specs=[anywhere] * 4 + [smem] * 2,
        out_specs=(anywhere, anywhere),
        scratch_shapes=[
            pltpu.VMEM((shards, d, tokens), BF16),
            pltpu.VMEM((shards, d, tokens), BF16),
            pltpu.VMEM((d, d), F32),
            pltpu.VMEM((d, d), F32),
            pltpu.VMEM((d, d), BF16),
            pltpu.VMEM((width, d), F32),
            pltpu.VMEM((width, d), BF16),
            pltpu.VMEM((height, d), F32),
            pltpu.VMEM((shards, width, tokens), BF16),
            pltpu.VMEM((d, width), F32),
            pltpu.VMEM(packed, BF16),
            pltpu.VMEM((height, width), BF16),
            pltpu.VMEM((height, width), F32),
            pltpu.VMEM((shards * tensors, 1, 128), F32),
            dma((5 + shards,)),
            dma,
            dma,
        ]
        + sems
        + [dma((PLANES, 2))] * 4,
        compiler_params=pltpu.CompilerParams(
            collective_id=0, has_side_effects=True, vmem_limit_bytes=62 * 2**20
        ),
    )(acts.T, outgrads.T, weight, momentum, damping, coeffs)
    new_momentum, gathered = pl.pallas_call(
        finish_kernel,
        out_shape=(
            jax.ShapeDtypeStruct((height, width), F32),
            jax.ShapeDtypeStruct((width, d), BF16),
        ),
        in_specs=[vmem, vmem],
        out_specs=(vmem, vmem),
    )(new_momentum, weights)
    return new_momentum, gathered.T


def solution(mesh):
    in_specs = (
        P("shard", "tensor"),
        P("shard", "tensor"),
        P("shard", "tensor"),
        P("shard", "tensor"),
        P(),
        P(),
    )
    out_specs = (P("shard", "tensor"), P(None, "tensor"))
    shape = (mesh.shape["shard"], mesh.shape["tensor"])
    whole = shape == (Y_CHIPS * PLANES, X_CHIPS * CORES)

    def local(acts, *rest):
        held = 2 * acts.dtype.itemsize * acts.size * shape[0] * shape[1]
        if whole and held <= 24 * 2**20:
            return on_device_whole(acts, *rest)
        return on_device(acts, *rest)

    return jax.shard_map(
        local, mesh=mesh, in_specs=in_specs, out_specs=out_specs, check_vma=False
    )
```

```python
import functools
import itertools

import jax
import jax.numpy as jnp
from jax import lax
from jax.experimental import pallas as pl
from jax.experimental.pallas import tpu as pltpu
from jax.sharding import PartitionSpec as P

D = 1152


def horner_columns(factor, coeffs, first_col, col_count, bound_norm):
    extent = factor.shape[0]
    row_ids = lax.broadcasted_iota(jnp.int32, (extent, col_count), 0)
    col_ids = lax.broadcasted_iota(jnp.int32, (extent, col_count), 1) + first_col
    identity_cols = (row_ids == col_ids).astype(jnp.float32)
    term_count = coeffs.shape[0]
    iterate = coeffs[term_count - 1] * identity_cols
    for term_index in range(term_count - 2, -1, -1):
        product = jnp.dot(factor, iterate.astype(jnp.bfloat16), preferred_element_type=jnp.float32)
        iterate = coeffs[term_index] * identity_cols + iterate - product / bound_norm
    return iterate


def tokens_product(left, right):
    return lax.dot_general(
        left, right, (((0,), (0,)), ((), ())), preferred_element_type=jnp.float32
    )


def on_device(acts, outgrads, weight, momentum, damping, coeffs):
    row_count = weight.shape[0]
    col_count = weight.shape[1]
    row_first = lax.axis_index("shard") * row_count
    col_first = lax.axis_index("tensor") * col_count
    full_acts, full_grads = (
        lax.all_gather(acts, "tensor", axis=1, tiled=True),
        lax.all_gather(outgrads, "tensor", axis=1, tiled=True),
    )
    local_squares = jnp.stack(
        [
            jnp.sum(jnp.square(acts.astype(jnp.float32))),
            jnp.sum(jnp.square(outgrads.astype(jnp.float32))),
        ]
    )
    traces = lax.psum(local_squares, ("shard", "tensor"))
    act_part = tokens_product(full_acts, acts)
    grad_part = tokens_product(full_grads, outgrads)
    stats = lax.psum_scatter(
        jnp.concatenate([act_part, grad_part], axis=1), "shard", scatter_dimension=0, tiled=True
    )
    row_ids = lax.broadcasted_iota(jnp.int32, (row_count, col_count), 0) + row_first
    col_ids = lax.broadcasted_iota(jnp.int32, (row_count, col_count), 1) + col_first
    diag_mask = (row_ids == col_ids).astype(jnp.float32)
    act_piece = (stats[:, :col_count] + damping[0] * traces[0] / D * diag_mask).astype(jnp.bfloat16)
    grad_piece = (stats[:, col_count:] + damping[1] * traces[1] / D * diag_mask).astype(
        jnp.bfloat16
    )
    act_wide, grad_wide = (
        lax.all_gather(act_piece, "tensor", axis=1, tiled=True),
        lax.all_gather(grad_piece, "tensor", axis=1, tiled=True),
    )
    act_full, grad_full = (
        lax.all_gather(act_wide, "shard", axis=0, tiled=True),
        lax.all_gather(grad_wide, "shard", axis=0, tiled=True),
    )
    act_scale = jnp.sqrt(jnp.sum(jnp.square(act_full.astype(jnp.float32))))
    grad_scale = jnp.sqrt(jnp.sum(jnp.square(grad_full.astype(jnp.float32))))
    act_inverse = horner_columns(act_full, coeffs, row_first, row_count, act_scale)
    grad_inverse = horner_columns(grad_full, coeffs, col_first, col_count, grad_scale).astype(
        jnp.bfloat16
    )
    projected = jnp.dot(full_grads, grad_inverse, preferred_element_type=jnp.float32).astype(
        jnp.bfloat16
    )
    right_term = tokens_product(full_acts, projected)
    right_product = lax.psum(right_term, "shard")
    update = lax.dot_general(
        act_inverse,
        right_product,
        (((0,), (0,)), ((), ())),
        precision=lax.Precision.HIGHEST,
        preferred_element_type=jnp.float32,
    )
    square_sum = lax.psum(jnp.sum(update * update), ("shard", "tensor"))
    mean_square = square_sum / (D * D)
    new_momentum = 0.9 * momentum + update / jnp.sqrt(mean_square + 1e-06)
    new_weight = (weight.astype(jnp.float32) - 0.1 * new_momentum).astype(jnp.bfloat16)
    gathered_weight = lax.all_gather(new_weight, "shard", axis=0, tiled=True)
    return (new_momentum, gathered_weight)


MESH = pl.DeviceIdType.MESH
BF16 = jnp.bfloat16
F32 = jnp.float32
X_CHIPS = 2
Y_CHIPS = 2
CORES = 2
TILES = 3
PLANES = 4
PARTS = 2


def dot_nt(left, right):
    return lax.dot_general(
        left, right, (((1,), (1,)), ((), ())), preferred_element_type=jnp.float32
    )


def dot_nn(left, right, precision=None):
    return lax.dot_general(
        left,
        right,
        (((1,), (0,)), ((), ())),
        precision=precision,
        preferred_element_type=jnp.float32,
    )


def eye(rows, cols, row_first, col_first):
    row_ids = lax.broadcasted_iota(jnp.int32, (rows, cols), 0) + row_first
    col_ids = lax.broadcasted_iota(jnp.int32, (rows, cols), 1) + col_first
    return row_ids == col_ids


def total(value):
    return jnp.sum(jnp.sum(value, axis=0, keepdims=True), axis=1, keepdims=True)


class Place:
    def __init__(self):
        self.s = lax.axis_index("shard")
        self.t = lax.axis_index("tensor")
        self.z, self.y = self.s // Y_CHIPS, self.s % Y_CHIPS
        self.x, self.c = self.t // CORES, self.t % CORES
        z, y, x, c = self.z, self.y, self.x, self.c
        self.mid = ((z + 1) // 2) % 2
        self.own = (y, x)
        self.p = (c * (1 - y) + (1 - c) * y, (1 - c) * (1 - x) + c * x)
        self.q = ((1 - c) * (1 - y) + c * y, c * (1 - x) + (1 - c) * x)
        self.d = (1 - y, 1 - x)

    def id(self, z, chip, c):
        return (z * Y_CHIPS + chip[0], chip[1] * CORES + c)

    def plane(self, k):
        z = self.z
        if isinstance(k, int):
            return [z, z + 1 - 2 * (z % 2), (z + 2) % PLANES, PLANES - 1 - z][k]
        return (k - 2) * (PLANES - 1 - z) + (3 - k) * ((z + 2) % PLANES)

    def slab(self, far, j):
        return self.plane(self.nth(j)) * Y_CHIPS + [self.y, 1 - self.y][far]

    def nth(self, j):
        return [0, 1, 2 + self.mid, 3 - self.mid][j]


class Stream:
    SLOTS = {"L": (8, 4), "P": (4, 4), "Q": (4, 4), "D": (8, 4)}

    def __init__(self, place, buf, width, first, count, sems):
        self.at, self.buf, self.width = place, buf, width
        self.first, self.count, self.sems = first, count, sems

    def block(self, k, chip, c):
        p = self.at
        rows = pl.multiple_of((c * X_CHIPS + chip[1]) * self.width + self.first, 16)
        return self.buf.at[p.plane(k) * Y_CHIPS + chip[0], pl.ds(rows, self.count), :]

    def copy(self, kind, index, ref, target, slot=None):
        send, recv = self.sems[kind]
        return pltpu.make_async_remote_copy(
            src_ref=ref,
            dst_ref=ref,
            send_sem=send.at[index if slot is None else slot],
            recv_sem=recv.at[index],
            device_id=target,
            device_id_type=MESH,
        )

    def arrive(self, kind, index, ref):
        p = self.at
        self.copy(kind, index, ref, p.id(p.z, p.own, 1 - p.c), 0).wait_recv()

    def to_p(self, kind, index, ref):
        p = self.at
        self.copy(kind, index, ref, p.id(p.z, p.p, p.c)).start()

    def to_q(self, kind, index, ref):
        p = self.at
        self.copy(kind, index, ref, p.id(p.z, p.q, p.c)).start()

    def to_plane(self, kind, index, ref, k, slot):
        p = self.at
        self.copy(kind, index, ref, p.id(p.plane(k), p.own, p.c), slot).start()

    def mid_to_plane(self, kind, index, ref, k, slot):
        @pl.when(self.at.mid == 1)
        def _():
            self.to_plane(kind, index, ref, k, slot)

    def own(self):
        p = self.at
        return self.block(0, p.own, p.c)

    def own_across(self):
        self.to_p("P", 0, self.own())
        self.to_q("Q", 0, self.own())

    def own_along(self):
        self.to_plane("L", 1, self.own(), 1, 1)
        self.mid_to_plane("L", 3, self.own(), 3, 3)

    def line(self, j):
        p = self.at
        k = p.nth(j)
        ref = self.block(k, p.own, p.c)
        self.arrive("L", k, ref)
        if j == 1:
            self.mid_to_plane("L", 2, ref, 3, 2)
        elif j == 2:
            self.mid_to_plane("L", 2, ref, 1, 6)
        else:
            self.mid_to_plane("L", 3, ref, 1, 7)
        self.to_p("P", k, ref)
        self.to_q("Q", k, ref)

    def pcol(self, j):
        p = self.at
        k = p.nth(j)
        ref = self.block(k, p.p, p.c)
        self.arrive("P", k, ref)
        if j == 3:
            self.to_q("D", k, ref)

    def qcol(self, j):
        p = self.at
        k = p.nth(j)
        ref = self.block(k, p.q, p.c)
        self.arrive("Q", k, ref)
        if j == 0:
            self.to_p("D", 0, ref)

    def diag(self, j):
        p = self.at
        k = p.nth(j)
        ref = self.block(k, p.d, p.c)
        self.arrive("D", k, ref)
        if j == 0:
            self.to_plane("D", 1, ref, 1, 5)
            self.mid_to_plane("D", 3, ref, 3, 7)
        if j == 2:
            self.mid_to_plane("D", 2, ref, 1, 6)

    def finish(self):
        p = self.at

        def sent(kind, slot):
            self.copy(kind, 0, self.own(), p.id(p.z, p.own, 1 - p.c), slot).wait_send()

        for k in range(4):
            sent("P", k)
            sent("Q", k)
        sent("L", 1)
        sent("D", 0)
        sent("D", 3 - p.mid)
        sent("D", 5)

        @pl.when(p.mid == 1)
        def _():
            for slot in (2, 3, 6, 7):
                sent("L", slot)
            for slot in (6, 7):
                sent("D", slot)


class Sibling:
    def __init__(self, place, buf, sems):
        self.at, self.buf, self.sems = place, buf, sems

    def copy(self, far, j, c):
        p = self.at
        k = p.nth(j)
        half = self.buf.shape[1] // CORES
        rows = pl.multiple_of(c * half, 16)
        ref = self.buf.at[p.slab(far, j), pl.ds(rows, half), :]
        return pltpu.make_async_remote_copy(
            src_ref=ref,
            dst_ref=ref,
            send_sem=self.sems[0].at[PLANES * far + k],
            recv_sem=self.sems[1].at[PLANES * far + k],
            device_id=p.id(p.z, p.own, 1 - p.c),
            device_id_type=MESH,
        )

    def send(self, far, j):
        self.copy(far, j, self.at.c).start()

    def arrive(self, far, j):
        self.copy(far, j, 1 - self.at.c).wait_recv()

    def finish(self):
        for far in range(2):
            for j in range(PLANES):
                self.copy(far, j, self.at.c).wait_send()


def cov_slab(buf, cov, slab, add):
    tile = cov.shape[0] // TILES
    for i in range(TILES):
        for j in range(i, TILES):
            rows, cols = pl.ds(i * tile, tile), pl.ds(j * tile, tile)
            product = dot_nt(buf[slab, rows, :], buf[slab, cols, :])
            cov[rows, cols] = cov[rows, cols] + product if add else product


def right_slab(buf, projected, right, slab, add):
    tile = right.shape[0] // TILES
    for i in range(TILES):
        rows = pl.ds(i * tile, tile)
        product = dot_nt(buf[slab, rows, :], projected[slab])
        right[rows, :] = right[rows, :] + product if add else product


def damp(cov, factor, damping):
    d = cov.shape[0]
    step = d // 9
    trace = jnp.zeros((1, 1), F32)
    for i in range(9):
        part = cov[i * step : (i + 1) * step, i * step : (i + 1) * step]
        trace = trace + total(jnp.where(eye(step, step, 0, 0), part, 0.0))
    shift = damping * trace / d

    tile = d // TILES
    unit = eye(tile, tile, 0, 0)
    ones = unit.astype(F32).astype(BF16)
    squares = jnp.zeros((1, tile), F32)
    for i in range(TILES):
        for j in range(i, TILES):
            rows, cols = slice(i * tile, (i + 1) * tile), slice(j * tile, (j + 1) * tile)
            piece = cov[rows, cols]
            if i == j:
                piece = piece + jnp.where(unit, shift, 0.0)
            low = piece.astype(BF16)
            factor[rows, cols] = low
            wide = low.astype(F32)
            square = jnp.sum(wide * wide, axis=0, keepdims=True)
            squares = squares + (square if i == j else 2.0 * square)
            if i != j:
                factor[cols, rows] = dot_nt(ones, low).astype(BF16)
    return jnp.sqrt(jnp.sum(squares, axis=1, keepdims=True))


def horner_steps(factor, work, coeffs, first, norm):
    rows, d = work.shape
    tile = d // TILES
    terms = coeffs.shape[0]

    def begin():
        start = pl.multiple_of(first, rows)
        top = jnp.full((1, 1), coeffs[terms - 1], F32).astype(BF16).astype(F32)
        diag = eye(rows, d, first, 0)
        value = jnp.where(diag, coeffs[terms - 2] + coeffs[terms - 1], 0.0)
        work[...] = value - factor[pl.ds(start, rows), :].astype(F32) * (top / norm())

    def term(index):
        low = work[...].astype(BF16)
        inv = 1.0 / norm()
        for j in range(TILES):
            cols = slice(j * tile, (j + 1) * tile)
            product = dot_nn(low, factor[:, cols])
            held = jnp.where(eye(rows, tile, first, j * tile), coeffs[index], 0.0)
            work[:, cols] = held + work[:, cols] - product * inv

    return [begin] + [functools.partial(term, k) for k in range(terms - 3, -1, -1)]


PLAN = [
    "GZ GX AZ AX",
    "GQ0m GQ0e GO2m GP0e",
    "GO1m GD0m GO3m GO1e",
    "AP0e AQ0m AQ0e GP0m",
    "GD0e AO1m GD2m GF0m",
    "GF0e GO2e AN0e GN0m",
    "AP0m GP2m GP1m GQ1m",
    "GD1e GP1e AN0m GQ2m",
    "AD0e GN1m GQ1e GF1e",
    "GF2m GN1e GO3e GQ2e",
    "AO1e GN0e GD1m GP2e",
    "GN2m an0 GF1m GP3m",
    "AO3m GQ3m gf0 AF0e",
    "gn1 GN3m GQ3e AO2m",
    "GD2e GF2e AD0m gn0",
    "GP3e gf1 AD1m AF0m",
    "gf2 AP1e GN3e GN2e",
    "AO3e AP1m AQ1m AN1m",
    "af0 AQ1e gn3 GD3m",
    "GD3e GF3e GF3m gn2",
    "AD2m AN1e AO2e gf3",
    "gd AQ3m AP3m AP3e",
    "h0 h1 h2 AN3m",
    "hl an1 AF1m AD1e",
    "AQ3e AN3e AF1e AP2e",
    "p0 p2 AQ2m AP2m",
    "p1 p3 AQ2e rn0",
    "AN2m AF2m rn1 rf0",
    "AN2e fg AD3m AD2e",
    "AF2e an3 AD3e AF3e",
    "rn3 af1 AF3m an2",
    "af2 rn2 af3 rf1",
    "rf3 rf2",
]


def step_kernel(
    acts_ref,
    grads_ref,
    weight_ref,
    momentum_ref,
    damping_ref,
    coeffs_ref,
    new_momentum_ref,
    weights_ref,
    acts_all,
    grads_all,
    cov,
    act_cov,
    factor,
    grad_work,
    grad_low,
    act_work,
    projected,
    right,
    weight_all,
    weight_own,
    momentum,
    sums,
    local_sems,
    sum_send,
    sum_recv,
    *sems,
):
    p = Place()
    s, t = p.s, p.t
    shards, tensors = Y_CHIPS * PLANES, X_CHIPS * CORES
    width = grads_ref.shape[0]
    height, d = weight_ref.shape[0], cov.shape[0]
    barrier = pltpu.get_barrier_semaphore()
    others = []
    for k in range(1, shards * tensors):
        others.append(((s + k // tensors) % shards, (t + k % tensors) % tensors))
    greeted = [p.id(p.z, p.p, p.c), p.id(p.z, p.q, p.c), p.id(p.z, p.own, 1 - p.c)]
    greeted += [p.id(p.plane(k), p.own, p.c) for k in range(1, PLANES)]
    for other in greeted:
        pl.semaphore_signal(barrier, inc=1, device_id=other, device_id_type=MESH)

    place = p.c * X_CHIPS + p.x
    own_rows = pl.ds(pl.multiple_of(place * width, width), width)
    loads = []
    for k, (src, dst) in enumerate(
        [
            (grads_ref, grads_all.at[s, own_rows, :]),
            (acts_ref, acts_all.at[s, own_rows, :]),
            (weight_ref, weight_own),
            (momentum_ref, momentum),
        ]
    ):
        loads.append(pltpu.make_async_copy(src, dst, local_sems.at[k]))
        loads[-1].start()

    pairs = list(zip(sems[0::2], sems[1::2]))
    kinds = list(Stream.SLOTS)
    part = width // PARTS
    streams, siblings = {}, {}
    for name, buf in (("G", grads_all), ("A", acts_all)):
        streams[name] = []
        for k in range(PARTS):
            own = dict(zip(kinds, pairs[: len(kinds)]))
            pairs = pairs[len(kinds) :]
            streams[name].append(Stream(p, buf, width, k * part, part, own))
        siblings[name] = Sibling(p, buf, pairs[0])
        pairs = pairs[1:]
    line_pair, cross_pair = pairs

    loads[0].wait()
    loads[1].wait()
    pl.semaphore_wait(barrier, len(greeted))

    def relay(word):
        if word[1] in "NF":
            siblings[word[0]].send("NF".index(word[1]), int(word[2]))
            return
        for stream in streams[word[0]]:
            if word[1] in "XZ":
                {"X": stream.own_across, "Z": stream.own_along}[word[1]]()
            else:
                move = {"O": stream.line, "P": stream.pcol, "Q": stream.qcol, "D": stream.diag}[word[1]]
                move(int(word[2]))

    def settle(name):
        siblings[name].finish()
        for stream in streams[name]:
            stream.finish()

    norms = {}
    horner_g = horner_steps(factor, grad_work, coeffs_ref, place * width, lambda: norms["g"])
    started = set()

    def compute(word):
        kind = word[0]
        if word == "fg":
            settle("G")
        elif word == "gd":
            norms["g"] = damp(cov, factor, damping_ref[1])
        elif word == "hl":
            grad_low[...] = grad_work[...].astype(BF16)
        elif kind == "h":
            horner_g[int(word[1])]()
        elif kind == "p":
            for k in (2 * int(word[1]), 2 * int(word[1]) + 1):
                projected[k] = dot_nn(grad_low[...], grads_all[k]).astype(BF16)
        else:
            far, j = "nf".index(word[1]), int(word[2])
            slab = p.slab(far, j)
            add = kind in started
            started.add(kind)
            if kind == "r":
                right_slab(acts_all, projected, right, slab, add)
            else:
                name = kind.upper()
                siblings[name].arrive(far, j)
                buf, out = {"G": (grads_all, cov), "A": (acts_all, act_cov)}[name]
                cov_slab(buf, out, slab, add)

    def group_of(word):
        if word[0] not in "GA":
            return word
        return word[-1] if word[-1] in "em" else "all"

    for group, words in itertools.groupby(" ".join(PLAN).split(), group_of):
        if group == "all":
            for word in words:
                relay(word)
        elif group in ("e", "m"):

            @pl.when(p.mid == "em".index(group))
            def _():
                for word in words:
                    relay(word[:-1])
        else:
            compute(group)

    act_norm = damp(act_cov, factor, damping_ref[0])
    block, inner = s * height // width, s * height % width
    first = (block % CORES * X_CHIPS + block // CORES) * width + inner
    for run in horner_steps(factor, act_work, coeffs_ref, first, lambda: act_norm):
        run()
    update = dot_nn(act_work[...], right[...], lax.Precision.HIGHEST)

    me = s * tensors + t
    sums[me] = jnp.broadcast_to(total(update * update), sums.shape[1:])
    count = shards * tensors
    for k, other in enumerate(others):
        pltpu.make_async_remote_copy(
            src_ref=sums.at[me],
            dst_ref=sums.at[me],
            send_sem=sum_send,
            recv_sem=sum_recv,
            device_id=other,
            device_id_type=MESH,
        ).start()
    loads[2].wait()
    loads[3].wait()
    settle("A")
    everyone = pltpu.make_async_remote_copy(
        src_ref=sums.at[: count - 1],
        dst_ref=sums.at[: count - 1],
        send_sem=sum_send,
        recv_sem=sum_recv,
        device_id=others[0],
        device_id_type=MESH,
    )
    everyone.wait_recv()
    square_sum = jnp.sum(sums[...], axis=0)[:, 0:1]
    mean_square = square_sum / (d * d)
    new = 0.9 * momentum[...] + update / jnp.sqrt(mean_square + 1e-06)
    momentum[...] = new
    low = (weight_own[...].astype(F32) - 0.1 * new).astype(BF16)
    main = weight_all.shape[2]
    rest = width - main
    weight_all[s, :height, :] = low[:, :main]
    ones = eye(rest, rest, 0, 0).astype(F32).astype(BF16)
    weight_all[s, height:, :height] = dot_nt(ones, low[:, main:]).astype(BF16)

    sent = []
    cuts = [slice(0, 96), slice(96, weight_all.shape[1])]

    def push(slab, pair, k, cut, target):
        part = weight_all.at[slab, cuts[cut], :]
        copy = pltpu.make_async_remote_copy(
            src_ref=part,
            dst_ref=part,
            send_sem=pair[0].at[k, cut],
            recv_sem=pair[1].at[k, cut],
            device_id=target,
            device_id_type=MESH,
        )
        copy.start()
        sent.append(copy)
        return copy

    across = (p.z * Y_CHIPS + 1 - p.y, t)
    order = [p.nth(j) for j in range(PLANES - 1, 0, -1)]
    crossed, lines = [], []
    for cut in range(len(cuts)):
        crossed.append((0, push(s, cross_pair, 0, cut, across)))
        for k in order:
            lines.append((k, cut, push(s, line_pair, k, cut, (p.plane(k) * Y_CHIPS + p.y, t))))
    stores = [pltpu.make_async_copy(momentum, new_momentum_ref, local_sems.at[4])]
    stores[0].start()

    def keep(slab):
        stores.append(
            pltpu.make_async_copy(
                weight_all.at[slab], weights_ref.at[slab], local_sems.at[4 + len(stores)]
            )
        )
        stores[-1].start()

    keep(s)
    for k in order:
        slab = p.plane(k) * Y_CHIPS + p.y
        for j, cut, copy in lines:
            if j is k:
                copy.wait_recv()
                crossed.append((k, push(slab, cross_pair, k, cut, across)))
        keep(slab)
    for k in [0] + order:
        for j, copy in crossed:
            if j is k:
                copy.wait_recv()
        keep(p.plane(k) * Y_CHIPS + 1 - p.y)
    for copy in sent:
        copy.wait_send()
    everyone.wait_send()
    for copy in stores:
        copy.wait()


def finish_kernel(momentum_ref, weights_ref, new_momentum_ref, gathered_ref):
    shards, rows, main = weights_ref.shape
    width = gathered_ref.shape[0]
    height = rows - (width - main)
    new_momentum_ref[...] = momentum_ref[...]
    low = jnp.concatenate([weights_ref[k, :height, :] for k in range(shards)], axis=0)
    ones = eye(main, main, 0, 0).astype(F32).astype(BF16)
    gathered_ref[:main, :] = dot_nt(ones, low).astype(BF16)
    for k in range(shards):
        gathered_ref[main:, k * height : (k + 1) * height] = weights_ref[k, height:, :height]


def on_device_whole(acts, outgrads, weight, momentum, damping, coeffs):
    tokens, width = acts.shape
    height = weight.shape[0]
    shards, tensors = Y_CHIPS * PLANES, X_CHIPS * CORES
    d = width * tensors
    main = width // 128 * 128
    packed = (shards, height + width - main, main)
    vmem = pl.BlockSpec(memory_space=pltpu.VMEM)
    smem = pl.BlockSpec(memory_space=pltpu.SMEM)
    anywhere = pl.BlockSpec(memory_space=pl.ANY)
    dma = pltpu.SemaphoreType.DMA
    sems = []
    for _ in range(2):
        for pair in list(Stream.SLOTS.values()) * PARTS + [(CORES * PLANES, CORES * PLANES)]:
            sems += [dma((count,)) for count in pair]
    new_momentum, weights = pl.pallas_call(
        step_kernel,
        out_shape=(
            jax.ShapeDtypeStruct((height, width), F32),
            jax.ShapeDtypeStruct(packed, BF16),
        ),
        in_specs=[anywhere] * 4 + [smem] * 2,
        out_specs=(anywhere, anywhere),
        scratch_shapes=[
            pltpu.VMEM((shards, d, tokens), BF16),
            pltpu.VMEM((shards, d, tokens), BF16),
            pltpu.VMEM((d, d), F32),
            pltpu.VMEM((d, d), F32),
            pltpu.VMEM((d, d), BF16),
            pltpu.VMEM((width, d), F32),
            pltpu.VMEM((width, d), BF16),
            pltpu.VMEM((height, d), F32),
            pltpu.VMEM((shards, width, tokens), BF16),
            pltpu.VMEM((d, width), F32),
            pltpu.VMEM(packed, BF16),
            pltpu.VMEM((height, width), BF16),
            pltpu.VMEM((height, width), F32),
            pltpu.VMEM((shards * tensors, 1, 128), F32),
            dma((5 + shards,)),
            dma,
            dma,
        ]
        + sems
        + [dma((PLANES, 2))] * 4,
        compiler_params=pltpu.CompilerParams(
            collective_id=0, has_side_effects=True, vmem_limit_bytes=62 * 2**20
        ),
    )(acts.T, outgrads.T, weight, momentum, damping, coeffs)
    new_momentum, gathered = pl.pallas_call(
        finish_kernel,
        out_shape=(
            jax.ShapeDtypeStruct((height, width), F32),
            jax.ShapeDtypeStruct((width, d), BF16),
        ),
        in_specs=[vmem, vmem],
        out_specs=(vmem, vmem),
    )(new_momentum, weights)
    return new_momentum, gathered.T


def solution(mesh):
    in_specs = (
        P("shard", "tensor"),
        P("shard", "tensor"),
        P("shard", "tensor"),
        P("shard", "tensor"),
        P(),
        P(),
    )
    out_specs = (P("shard", "tensor"), P(None, "tensor"))
    shape = (mesh.shape["shard"], mesh.shape["tensor"])
    whole = shape == (Y_CHIPS * PLANES, X_CHIPS * CORES)

    def local(acts, *rest):
        held = 2 * acts.dtype.itemsize * acts.size * shape[0] * shape[1]
        if whole and held <= 24 * 2**20:
            return on_device_whole(acts, *rest)
        return on_device(acts, *rest)

    return jax.shard_map(
        local, mesh=mesh, in_specs=in_specs, out_specs=out_specs, check_vma=False
    )
```

```python
import functools
import itertools

import jax
import jax.numpy as jnp
from jax import lax
from jax.experimental import pallas as pl
from jax.experimental.pallas import tpu as pltpu
from jax.sharding import PartitionSpec as P

D = 1152


def horner_columns(factor, coeffs, first_col, col_count, bound_norm):
    extent = factor.shape[0]
    row_ids = lax.broadcasted_iota(jnp.int32, (extent, col_count), 0)
    col_ids = lax.broadcasted_iota(jnp.int32, (extent, col_count), 1) + first_col
    identity_cols = (row_ids == col_ids).astype(jnp.float32)
    term_count = coeffs.shape[0]
    iterate = coeffs[term_count - 1] * identity_cols
    for term_index in range(term_count - 2, -1, -1):
        product = jnp.dot(factor, iterate.astype(jnp.bfloat16), preferred_element_type=jnp.float32)
        iterate = coeffs[term_index] * identity_cols + iterate - product / bound_norm
    return iterate


def tokens_product(left, right):
    return lax.dot_general(
        left, right, (((0,), (0,)), ((), ())), preferred_element_type=jnp.float32
    )


def on_device(acts, outgrads, weight, momentum, damping, coeffs):
    row_count = weight.shape[0]
    col_count = weight.shape[1]
    row_first = lax.axis_index("shard") * row_count
    col_first = lax.axis_index("tensor") * col_count
    full_acts, full_grads = (
        lax.all_gather(acts, "tensor", axis=1, tiled=True),
        lax.all_gather(outgrads, "tensor", axis=1, tiled=True),
    )
    local_squares = jnp.stack(
        [
            jnp.sum(jnp.square(acts.astype(jnp.float32))),
            jnp.sum(jnp.square(outgrads.astype(jnp.float32))),
        ]
    )
    traces = lax.psum(local_squares, ("shard", "tensor"))
    act_part = tokens_product(full_acts, acts)
    grad_part = tokens_product(full_grads, outgrads)
    stats = lax.psum_scatter(
        jnp.concatenate([act_part, grad_part], axis=1), "shard", scatter_dimension=0, tiled=True
    )
    row_ids = lax.broadcasted_iota(jnp.int32, (row_count, col_count), 0) + row_first
    col_ids = lax.broadcasted_iota(jnp.int32, (row_count, col_count), 1) + col_first
    diag_mask = (row_ids == col_ids).astype(jnp.float32)
    act_piece = (stats[:, :col_count] + damping[0] * traces[0] / D * diag_mask).astype(jnp.bfloat16)
    grad_piece = (stats[:, col_count:] + damping[1] * traces[1] / D * diag_mask).astype(
        jnp.bfloat16
    )
    act_wide, grad_wide = (
        lax.all_gather(act_piece, "tensor", axis=1, tiled=True),
        lax.all_gather(grad_piece, "tensor", axis=1, tiled=True),
    )
    act_full, grad_full = (
        lax.all_gather(act_wide, "shard", axis=0, tiled=True),
        lax.all_gather(grad_wide, "shard", axis=0, tiled=True),
    )
    act_scale = jnp.sqrt(jnp.sum(jnp.square(act_full.astype(jnp.float32))))
    grad_scale = jnp.sqrt(jnp.sum(jnp.square(grad_full.astype(jnp.float32))))
    act_inverse = horner_columns(act_full, coeffs, row_first, row_count, act_scale)
    grad_inverse = horner_columns(grad_full, coeffs, col_first, col_count, grad_scale).astype(
        jnp.bfloat16
    )
    projected = jnp.dot(full_grads, grad_inverse, preferred_element_type=jnp.float32).astype(
        jnp.bfloat16
    )
    right_term = tokens_product(full_acts, projected)
    right_product = lax.psum(right_term, "shard")
    update = lax.dot_general(
        act_inverse,
        right_product,
        (((0,), (0,)), ((), ())),
        precision=lax.Precision.HIGHEST,
        preferred_element_type=jnp.float32,
    )
    square_sum = lax.psum(jnp.sum(update * update), ("shard", "tensor"))
    mean_square = square_sum / (D * D)
    new_momentum = 0.9 * momentum + update / jnp.sqrt(mean_square + 1e-06)
    new_weight = (weight.astype(jnp.float32) - 0.1 * new_momentum).astype(jnp.bfloat16)
    gathered_weight = lax.all_gather(new_weight, "shard", axis=0, tiled=True)
    return (new_momentum, gathered_weight)


MESH = pl.DeviceIdType.MESH
BF16 = jnp.bfloat16
F32 = jnp.float32
X_CHIPS = 2
Y_CHIPS = 2
CORES = 2
TILES = 3
PLANES = 4
PARTS = 2


def dot_nt(left, right):
    return lax.dot_general(
        left, right, (((1,), (1,)), ((), ())), preferred_element_type=jnp.float32
    )


def dot_nn(left, right, precision=None):
    return lax.dot_general(
        left,
        right,
        (((1,), (0,)), ((), ())),
        precision=precision,
        preferred_element_type=jnp.float32,
    )


def eye(rows, cols, row_first, col_first):
    row_ids = lax.broadcasted_iota(jnp.int32, (rows, cols), 0) + row_first
    col_ids = lax.broadcasted_iota(jnp.int32, (rows, cols), 1) + col_first
    return row_ids == col_ids


def total(value):
    return jnp.sum(jnp.sum(value, axis=0, keepdims=True), axis=1, keepdims=True)


class Place:
    def __init__(self):
        self.s = lax.axis_index("shard")
        self.t = lax.axis_index("tensor")
        self.z, self.y = self.s // Y_CHIPS, self.s % Y_CHIPS
        self.x, self.c = self.t // CORES, self.t % CORES
        z, y, x, c = self.z, self.y, self.x, self.c
        self.mid = ((z + 1) // 2) % 2
        self.own = (y, x)
        self.p = (c * (1 - y) + (1 - c) * y, (1 - c) * (1 - x) + c * x)
        self.q = ((1 - c) * (1 - y) + c * y, c * (1 - x) + (1 - c) * x)
        self.d = (1 - y, 1 - x)

    def id(self, z, chip, c):
        return (z * Y_CHIPS + chip[0], chip[1] * CORES + c)

    def plane(self, k):
        z = self.z
        if isinstance(k, int):
            return [z, z + 1 - 2 * (z % 2), (z + 2) % PLANES, PLANES - 1 - z][k]
        return (k - 2) * (PLANES - 1 - z) + (3 - k) * ((z + 2) % PLANES)

    def slab(self, far, j):
        return self.plane(self.nth(j)) * Y_CHIPS + [self.y, 1 - self.y][far]

    def nth(self, j):
        return [0, 1, 2 + self.mid, 3 - self.mid][j]


class Stream:
    SLOTS = {"L": (8, 4), "P": (4, 4), "Q": (4, 4), "D": (8, 4)}

    def __init__(self, place, buf, width, first, count, sems):
        self.at, self.buf, self.width = place, buf, width
        self.first, self.count, self.sems = first, count, sems

    def block(self, k, chip, c):
        p = self.at
        rows = pl.multiple_of((c * X_CHIPS + chip[1]) * self.width + self.first, 16)
        return self.buf.at[p.plane(k) * Y_CHIPS + chip[0], pl.ds(rows, self.count), :]

    def copy(self, kind, index, ref, target, slot=None):
        send, recv = self.sems[kind]
        return pltpu.make_async_remote_copy(
            src_ref=ref,
            dst_ref=ref,
            send_sem=send.at[index if slot is None else slot],
            recv_sem=recv.at[index],
            device_id=target,
            device_id_type=MESH,
        )

    def arrive(self, kind, index, ref):
        p = self.at
        self.copy(kind, index, ref, p.id(p.z, p.own, 1 - p.c), 0).wait_recv()

    def to_p(self, kind, index, ref):
        p = self.at
        self.copy(kind, index, ref, p.id(p.z, p.p, p.c)).start()

    def to_q(self, kind, index, ref):
        p = self.at
        self.copy(kind, index, ref, p.id(p.z, p.q, p.c)).start()

    def to_plane(self, kind, index, ref, k, slot):
        p = self.at
        self.copy(kind, index, ref, p.id(p.plane(k), p.own, p.c), slot).start()

    def mid_to_plane(self, kind, index, ref, k, slot):
        @pl.when(self.at.mid == 1)
        def _():
            self.to_plane(kind, index, ref, k, slot)

    def own(self):
        p = self.at
        return self.block(0, p.own, p.c)

    def own_across(self):
        self.to_p("P", 0, self.own())
        self.to_q("Q", 0, self.own())

    def own_along(self):
        self.to_plane("L", 1, self.own(), 1, 1)
        self.mid_to_plane("L", 3, self.own(), 3, 3)

    def line(self, j):
        p = self.at
        k = p.nth(j)
        ref = self.block(k, p.own, p.c)
        self.arrive("L", k, ref)
        if j == 1:
            self.mid_to_plane("L", 2, ref, 3, 2)
        elif j == 2:
            self.mid_to_plane("L", 2, ref, 1, 6)
        else:
            self.mid_to_plane("L", 3, ref, 1, 7)
        self.to_p("P", k, ref)
        self.to_q("Q", k, ref)

    def pcol(self, j):
        p = self.at
        k = p.nth(j)
        ref = self.block(k, p.p, p.c)
        self.arrive("P", k, ref)
        if j == 3:
            self.to_q("D", k, ref)

    def qcol(self, j):
        p = self.at
        k = p.nth(j)
        ref = self.block(k, p.q, p.c)
        self.arrive("Q", k, ref)
        if j == 0:
            self.to_p("D", 0, ref)

    def diag(self, j):
        p = self.at
        k = p.nth(j)
        ref = self.block(k, p.d, p.c)
        self.arrive("D", k, ref)
        if j == 0:
            self.to_plane("D", 1, ref, 1, 5)
            self.mid_to_plane("D", 3, ref, 3, 7)
        if j == 2:
            self.mid_to_plane("D", 2, ref, 1, 6)

    def finish(self):
        p = self.at

        def sent(kind, slot):
            self.copy(kind, 0, self.own(), p.id(p.z, p.own, 1 - p.c), slot).wait_send()

        for k in range(4):
            sent("P", k)
            sent("Q", k)
        sent("L", 1)
        sent("D", 0)
        sent("D", 3 - p.mid)
        sent("D", 5)

        @pl.when(p.mid == 1)
        def _():
            for slot in (2, 3, 6, 7):
                sent("L", slot)
            for slot in (6, 7):
                sent("D", slot)


class Sibling:
    def __init__(self, place, buf, sems):
        self.at, self.buf, self.sems = place, buf, sems

    def copy(self, far, j, c):
        p = self.at
        k = p.nth(j)
        half = self.buf.shape[1] // CORES
        rows = pl.multiple_of(c * half, 16)
        ref = self.buf.at[p.slab(far, j), pl.ds(rows, half), :]
        return pltpu.make_async_remote_copy(
            src_ref=ref,
            dst_ref=ref,
            send_sem=self.sems[0].at[PLANES * far + k],
            recv_sem=self.sems[1].at[PLANES * far + k],
            device_id=p.id(p.z, p.own, 1 - p.c),
            device_id_type=MESH,
        )

    def send(self, far, j):
        self.copy(far, j, self.at.c).start()

    def arrive(self, far, j):
        self.copy(far, j, 1 - self.at.c).wait_recv()

    def finish(self):
        for far in range(2):
            for j in range(PLANES):
                self.copy(far, j, self.at.c).wait_send()


def cov_slab(buf, cov, slab, add):
    tile = cov.shape[0] // TILES
    for i in range(TILES):
        for j in range(i, TILES):
            rows, cols = pl.ds(i * tile, tile), pl.ds(j * tile, tile)
            product = dot_nt(buf[slab, rows, :], buf[slab, cols, :])
            cov[rows, cols] = cov[rows, cols] + product if add else product


def right_slab(buf, projected, right, slab, add):
    tile = right.shape[0] // TILES
    for i in range(TILES):
        rows = pl.ds(i * tile, tile)
        product = dot_nt(buf[slab, rows, :], projected[slab])
        right[rows, :] = right[rows, :] + product if add else product


def damp(cov, factor, damping):
    d = cov.shape[0]
    step = d // 9
    trace = jnp.zeros((1, 1), F32)
    for i in range(9):
        part = cov[i * step : (i + 1) * step, i * step : (i + 1) * step]
        trace = trace + total(jnp.where(eye(step, step, 0, 0), part, 0.0))
    shift = damping * trace / d

    tile = d // TILES
    unit = eye(tile, tile, 0, 0)
    ones = unit.astype(F32).astype(BF16)
    squares = jnp.zeros((1, tile), F32)
    for i in range(TILES):
        for j in range(i, TILES):
            rows, cols = slice(i * tile, (i + 1) * tile), slice(j * tile, (j + 1) * tile)
            piece = cov[rows, cols]
            if i == j:
                piece = piece + jnp.where(unit, shift, 0.0)
            low = piece.astype(BF16)
            factor[rows, cols] = low
            wide = low.astype(F32)
            square = jnp.sum(wide * wide, axis=0, keepdims=True)
            squares = squares + (square if i == j else 2.0 * square)
            if i != j:
                factor[cols, rows] = dot_nt(ones, low).astype(BF16)
    return jnp.sqrt(jnp.sum(squares, axis=1, keepdims=True))


def horner_steps(factor, work, coeffs, first, norm):
    rows, d = work.shape
    tile = d // TILES
    terms = coeffs.shape[0]

    def begin():
        start = pl.multiple_of(first, rows)
        top = jnp.full((1, 1), coeffs[terms - 1], F32).astype(BF16).astype(F32)
        diag = eye(rows, d, first, 0)
        value = jnp.where(diag, coeffs[terms - 2] + coeffs[terms - 1], 0.0)
        work[...] = value - factor[pl.ds(start, rows), :].astype(F32) * (top / norm())

    def term(index):
        low = work[...].astype(BF16)
        inv = 1.0 / norm()
        for j in range(TILES):
            cols = slice(j * tile, (j + 1) * tile)
            product = dot_nn(low, factor[:, cols])
            held = jnp.where(eye(rows, tile, first, j * tile), coeffs[index], 0.0)
            work[:, cols] = held + work[:, cols] - product * inv

    return [begin] + [functools.partial(term, k) for k in range(terms - 3, -1, -1)]


PLAN = [
    "GZ GX AZ AX",
    "GQ0m GQ0e GO2m GP0e",
    "GO1m GD0m GO3m GO1e",
    "AP0e AQ0m AQ0e GP0m",
    "GD0e AO1m GD2m GF0m",
    "GF0e GO2e AN0e GN0m",
    "AP0m GP2m GP1m GQ1m",
    "GD1e GP1e AN0m GQ2m",
    "AD0e GN1m GQ1e GF1e",
    "GF2m GN1e GO3e GQ2e",
    "AO1e GN0e GD1m GP2e",
    "GN2m an0 GF1m GP3m",
    "AO3m GQ3m gf0 AF0e",
    "gn1 GN3m GQ3e AO2m",
    "GD2e GF2e AD0m gn0",
    "GP3e gf1 AD1m AF0m",
    "gf2 AP1e GN3e GN2e",
    "AO3e AP1m AQ1m AN1m",
    "af0 AQ1e gn3 GD3m",
    "GD3e GF3e GF3m gn2",
    "AD2m AN1e AO2e gf3",
    "gd AQ3m AP3m AP3e",
    "h0 h1 h2 AN3m",
    "hl an1 AF1m AD1e",
    "AQ3e AN3e AF1e AP2e",
    "p0 p2 AQ2m AP2m",
    "p1 p3 AQ2e rn0",
    "AN2m AF2m rn1 rf0",
    "AN2e fg AD3m AD2e",
    "AF2e an3 AD3e AF3e",
    "rn3 af1 AF3m an2",
    "af2 rn2 af3 rf1",
    "rf3 rf2",
]


def step_kernel(
    acts_ref,
    grads_ref,
    weight_ref,
    momentum_ref,
    damping_ref,
    coeffs_ref,
    new_momentum_ref,
    weights_ref,
    acts_all,
    grads_all,
    cov,
    act_cov,
    factor,
    grad_work,
    grad_low,
    act_work,
    projected,
    right,
    weight_all,
    weight_own,
    momentum,
    sums,
    local_sems,
    sum_send,
    sum_recv,
    *sems,
):
    p = Place()
    s, t = p.s, p.t
    shards, tensors = Y_CHIPS * PLANES, X_CHIPS * CORES
    width = grads_ref.shape[0]
    height, d = weight_ref.shape[0], cov.shape[0]
    barrier = pltpu.get_barrier_semaphore()
    others = []
    for hop in (4, 5, 3, 2, 6, 1, 7, 0):
        for k in range(tensors):
            if hop + k > 0:
                others.append(((s + hop) % shards, (t + k) % tensors))
    greeted = [p.id(p.z, p.p, p.c), p.id(p.z, p.q, p.c), p.id(p.z, p.own, 1 - p.c)]
    greeted += [p.id(p.plane(k), p.own, p.c) for k in range(1, PLANES)]
    for other in greeted:
        pl.semaphore_signal(barrier, inc=1, device_id=other, device_id_type=MESH)

    place = p.c * X_CHIPS + p.x
    own_rows = pl.ds(pl.multiple_of(place * width, width), width)
    loads = []
    for k, (src, dst) in enumerate(
        [
            (grads_ref, grads_all.at[s, own_rows, :]),
            (acts_ref, acts_all.at[s, own_rows, :]),
            (weight_ref, weight_own),
            (momentum_ref, momentum),
        ]
    ):
        loads.append(pltpu.make_async_copy(src, dst, local_sems.at[k]))
        loads[-1].start()

    pairs = list(zip(sems[0::2], sems[1::2]))
    kinds = list(Stream.SLOTS)
    part = width // PARTS
    streams, siblings = {}, {}
    for name, buf in (("G", grads_all), ("A", acts_all)):
        streams[name] = []
        for k in range(PARTS):
            own = dict(zip(kinds, pairs[: len(kinds)]))
            pairs = pairs[len(kinds) :]
            streams[name].append(Stream(p, buf, width, k * part, part, own))
        siblings[name] = Sibling(p, buf, pairs[0])
        pairs = pairs[1:]
    line_pair, cross_pair = pairs

    loads[0].wait()
    loads[1].wait()
    pl.semaphore_wait(barrier, len(greeted))

    def relay(word):
        if word[1] in "NF":
            siblings[word[0]].send("NF".index(word[1]), int(word[2]))
            return
        for stream in streams[word[0]]:
            if word[1] in "XZ":
                {"X": stream.own_across, "Z": stream.own_along}[word[1]]()
            else:
                move = {"O": stream.line, "P": stream.pcol, "Q": stream.qcol, "D": stream.diag}[word[1]]
                move(int(word[2]))

    def settle(name):
        siblings[name].finish()
        for stream in streams[name]:
            stream.finish()

    norms = {}
    horner_g = horner_steps(factor, grad_work, coeffs_ref, place * width, lambda: norms["g"])
    started = set()

    def compute(word):
        kind = word[0]
        if word == "fg":
            settle("G")
        elif word == "gd":
            norms["g"] = damp(cov, factor, damping_ref[1])
        elif word == "hl":
            grad_low[...] = grad_work[...].astype(BF16)
        elif kind == "h":
            horner_g[int(word[1])]()
        elif kind == "p":
            for k in (2 * int(word[1]), 2 * int(word[1]) + 1):
                projected[k] = dot_nn(grad_low[...], grads_all[k]).astype(BF16)
        else:
            far, j = "nf".index(word[1]), int(word[2])
            slab = p.slab(far, j)
            add = kind in started
            started.add(kind)
            if kind == "r":
                right_slab(acts_all, projected, right, slab, add)
            else:
                name = kind.upper()
                siblings[name].arrive(far, j)
                buf, out = {"G": (grads_all, cov), "A": (acts_all, act_cov)}[name]
                cov_slab(buf, out, slab, add)

    def group_of(word):
        if word[0] not in "GA":
            return word
        return word[-1] if word[-1] in "em" else "all"

    for group, words in itertools.groupby(" ".join(PLAN).split(), group_of):
        if group == "all":
            for word in words:
                relay(word)
        elif group in ("e", "m"):

            @pl.when(p.mid == "em".index(group))
            def _():
                for word in words:
                    relay(word[:-1])
        else:
            compute(group)

    act_norm = damp(act_cov, factor, damping_ref[0])
    block, inner = s * height // width, s * height % width
    first = (block % CORES * X_CHIPS + block // CORES) * width + inner
    for run in horner_steps(factor, act_work, coeffs_ref, first, lambda: act_norm):
        run()
    update = dot_nn(act_work[...], right[...], lax.Precision.HIGHEST)

    me = s * tensors + t
    sums[me] = jnp.broadcast_to(total(update * update), sums.shape[1:])
    count = shards * tensors
    for k, other in enumerate(others):
        pltpu.make_async_remote_copy(
            src_ref=sums.at[me],
            dst_ref=sums.at[me],
            send_sem=sum_send,
            recv_sem=sum_recv,
            device_id=other,
            device_id_type=MESH,
        ).start()
    loads[2].wait()
    loads[3].wait()
    settle("A")
    everyone = pltpu.make_async_remote_copy(
        src_ref=sums.at[: count - 1],
        dst_ref=sums.at[: count - 1],
        send_sem=sum_send,
        recv_sem=sum_recv,
        device_id=others[0],
        device_id_type=MESH,
    )
    everyone.wait_recv()
    square_sum = jnp.sum(sums[...], axis=0)[:, 0:1]
    mean_square = square_sum / (d * d)
    new = 0.9 * momentum[...] + update / jnp.sqrt(mean_square + 1e-06)
    momentum[...] = new
    low = (weight_own[...].astype(F32) - 0.1 * new).astype(BF16)
    main = weight_all.shape[2]
    rest = width - main
    weight_all[s, :height, :] = low[:, :main]
    ones = eye(rest, rest, 0, 0).astype(F32).astype(BF16)
    weight_all[s, height:, :height] = dot_nt(ones, low[:, main:]).astype(BF16)

    cuts = [slice(0, 96), slice(96, weight_all.shape[1])]

    def push(slab, pair, k, cut, target, into=weight_all):
        copy = pltpu.make_async_remote_copy(
            src_ref=weight_all.at[slab, cuts[cut], :],
            dst_ref=into.at[slab, cuts[cut], :],
            send_sem=pair[0].at[k, cut],
            recv_sem=pair[1].at[k, cut],
            device_id=target,
            device_id_type=MESH,
        )
        copy.start()
        return copy

    across = (p.z * Y_CHIPS + 1 - p.y, t)
    order = [p.nth(j) for j in range(PLANES - 1, 0, -1)]
    crossed, lines = [], []
    for cut in range(len(cuts)):
        crossed.append(push(s, cross_pair, 0, cut, across, weights_ref))
        for k in order:
            lines.append((k, cut, push(s, line_pair, k, cut, (p.plane(k) * Y_CHIPS + p.y, t))))
    stores = [pltpu.make_async_copy(momentum, new_momentum_ref, local_sems.at[4])]
    stores[0].start()

    def keep(slab):
        stores.append(
            pltpu.make_async_copy(
                weight_all.at[slab], weights_ref.at[slab], local_sems.at[4 + len(stores)]
            )
        )
        stores[-1].start()

    keep(s)
    for k in order:
        slab = p.plane(k) * Y_CHIPS + p.y
        for j, cut, copy in lines:
            if j is k:
                copy.wait_recv()
                crossed.append(push(slab, cross_pair, k, cut, across, weights_ref))
        keep(slab)
    everyone.wait_send()
    for _, _, copy in lines:
        copy.wait_send()
    for copy in stores:
        copy.wait()
    for copy in crossed:
        copy.wait()


def finish_kernel(momentum_ref, weights_ref, new_momentum_ref, gathered_ref):
    shards, rows, main = weights_ref.shape
    width = gathered_ref.shape[0]
    height = rows - (width - main)
    new_momentum_ref[...] = momentum_ref[...]
    low = jnp.concatenate([weights_ref[k, :height, :] for k in range(shards)], axis=0)
    ones = eye(main, main, 0, 0).astype(F32).astype(BF16)
    gathered_ref[:main, :] = dot_nt(ones, low).astype(BF16)
    for k in range(shards):
        gathered_ref[main:, k * height : (k + 1) * height] = weights_ref[k, height:, :height]


def on_device_whole(acts, outgrads, weight, momentum, damping, coeffs):
    tokens, width = acts.shape
    height = weight.shape[0]
    shards, tensors = Y_CHIPS * PLANES, X_CHIPS * CORES
    d = width * tensors
    main = width // 128 * 128
    packed = (shards, height + width - main, main)
    vmem = pl.BlockSpec(memory_space=pltpu.VMEM)
    smem = pl.BlockSpec(memory_space=pltpu.SMEM)
    anywhere = pl.BlockSpec(memory_space=pl.ANY)
    dma = pltpu.SemaphoreType.DMA
    sems = []
    for _ in range(2):
        for pair in list(Stream.SLOTS.values()) * PARTS + [(CORES * PLANES, CORES * PLANES)]:
            sems += [dma((count,)) for count in pair]
    new_momentum, weights = pl.pallas_call(
        step_kernel,
        out_shape=(
            jax.ShapeDtypeStruct((height, width), F32),
            jax.ShapeDtypeStruct(packed, BF16),
        ),
        in_specs=[anywhere] * 4 + [smem] * 2,
        out_specs=(anywhere, anywhere),
        scratch_shapes=[
            pltpu.VMEM((shards, d, tokens), BF16),
            pltpu.VMEM((shards, d, tokens), BF16),
            pltpu.VMEM((d, d), F32),
            pltpu.VMEM((d, d), F32),
            pltpu.VMEM((d, d), BF16),
            pltpu.VMEM((width, d), F32),
            pltpu.VMEM((width, d), BF16),
            pltpu.VMEM((height, d), F32),
            pltpu.VMEM((shards, width, tokens), BF16),
            pltpu.VMEM((d, width), F32),
            pltpu.VMEM(packed, BF16),
            pltpu.VMEM((height, width), BF16),
            pltpu.VMEM((height, width), F32),
            pltpu.VMEM((shards * tensors, 1, 128), F32),
            dma((5 + PLANES,)),
            dma,
            dma,
        ]
        + sems
        + [dma((PLANES, 2))] * 4,
        compiler_params=pltpu.CompilerParams(
            collective_id=0, has_side_effects=True, vmem_limit_bytes=62 * 2**20
        ),
    )(acts.T, outgrads.T, weight, momentum, damping, coeffs)
    new_momentum, gathered = pl.pallas_call(
        finish_kernel,
        out_shape=(
            jax.ShapeDtypeStruct((height, width), F32),
            jax.ShapeDtypeStruct((width, d), BF16),
        ),
        in_specs=[vmem, vmem],
        out_specs=(vmem, vmem),
    )(new_momentum, weights)
    return new_momentum, gathered.T


def solution(mesh):
    in_specs = (
        P("shard", "tensor"),
        P("shard", "tensor"),
        P("shard", "tensor"),
        P("shard", "tensor"),
        P(),
        P(),
    )
    out_specs = (P("shard", "tensor"), P(None, "tensor"))
    shape = (mesh.shape["shard"], mesh.shape["tensor"])
    whole = shape == (Y_CHIPS * PLANES, X_CHIPS * CORES)

    def local(acts, *rest):
        held = 2 * acts.dtype.itemsize * acts.size * shape[0] * shape[1]
        if whole and held <= 24 * 2**20:
            return on_device_whole(acts, *rest)
        return on_device(acts, *rest)

    return jax.shard_map(
        local, mesh=mesh, in_specs=in_specs, out_specs=out_specs, check_vma=False
    )
```

```python
import functools
import itertools

import jax
import jax.numpy as jnp
from jax import lax
from jax.experimental import pallas as pl
from jax.experimental.pallas import tpu as pltpu
from jax.sharding import PartitionSpec as P

D = 1152


def horner_columns(factor, coeffs, first_col, col_count, bound_norm):
    extent = factor.shape[0]
    row_ids = lax.broadcasted_iota(jnp.int32, (extent, col_count), 0)
    col_ids = lax.broadcasted_iota(jnp.int32, (extent, col_count), 1) + first_col
    identity_cols = (row_ids == col_ids).astype(jnp.float32)
    term_count = coeffs.shape[0]
    iterate = coeffs[term_count - 1] * identity_cols
    for term_index in range(term_count - 2, -1, -1):
        product = jnp.dot(factor, iterate.astype(jnp.bfloat16), preferred_element_type=jnp.float32)
        iterate = coeffs[term_index] * identity_cols + iterate - product / bound_norm
    return iterate


def tokens_product(left, right):
    return lax.dot_general(
        left, right, (((0,), (0,)), ((), ())), preferred_element_type=jnp.float32
    )


def on_device(acts, outgrads, weight, momentum, damping, coeffs):
    row_count = weight.shape[0]
    col_count = weight.shape[1]
    row_first = lax.axis_index("shard") * row_count
    col_first = lax.axis_index("tensor") * col_count
    full_acts, full_grads = (
        lax.all_gather(acts, "tensor", axis=1, tiled=True),
        lax.all_gather(outgrads, "tensor", axis=1, tiled=True),
    )
    local_squares = jnp.stack(
        [
            jnp.sum(jnp.square(acts.astype(jnp.float32))),
            jnp.sum(jnp.square(outgrads.astype(jnp.float32))),
        ]
    )
    traces = lax.psum(local_squares, ("shard", "tensor"))
    act_part = tokens_product(full_acts, acts)
    grad_part = tokens_product(full_grads, outgrads)
    stats = lax.psum_scatter(
        jnp.concatenate([act_part, grad_part], axis=1), "shard", scatter_dimension=0, tiled=True
    )
    row_ids = lax.broadcasted_iota(jnp.int32, (row_count, col_count), 0) + row_first
    col_ids = lax.broadcasted_iota(jnp.int32, (row_count, col_count), 1) + col_first
    diag_mask = (row_ids == col_ids).astype(jnp.float32)
    act_piece = (stats[:, :col_count] + damping[0] * traces[0] / D * diag_mask).astype(jnp.bfloat16)
    grad_piece = (stats[:, col_count:] + damping[1] * traces[1] / D * diag_mask).astype(
        jnp.bfloat16
    )
    act_wide, grad_wide = (
        lax.all_gather(act_piece, "tensor", axis=1, tiled=True),
        lax.all_gather(grad_piece, "tensor", axis=1, tiled=True),
    )
    act_full, grad_full = (
        lax.all_gather(act_wide, "shard", axis=0, tiled=True),
        lax.all_gather(grad_wide, "shard", axis=0, tiled=True),
    )
    act_scale = jnp.sqrt(jnp.sum(jnp.square(act_full.astype(jnp.float32))))
    grad_scale = jnp.sqrt(jnp.sum(jnp.square(grad_full.astype(jnp.float32))))
    act_inverse = horner_columns(act_full, coeffs, row_first, row_count, act_scale)
    grad_inverse = horner_columns(grad_full, coeffs, col_first, col_count, grad_scale).astype(
        jnp.bfloat16
    )
    projected = jnp.dot(full_grads, grad_inverse, preferred_element_type=jnp.float32).astype(
        jnp.bfloat16
    )
    right_term = tokens_product(full_acts, projected)
    right_product = lax.psum(right_term, "shard")
    update = lax.dot_general(
        act_inverse,
        right_product,
        (((0,), (0,)), ((), ())),
        precision=lax.Precision.HIGHEST,
        preferred_element_type=jnp.float32,
    )
    square_sum = lax.psum(jnp.sum(update * update), ("shard", "tensor"))
    mean_square = square_sum / (D * D)
    new_momentum = 0.9 * momentum + update / jnp.sqrt(mean_square + 1e-06)
    new_weight = (weight.astype(jnp.float32) - 0.1 * new_momentum).astype(jnp.bfloat16)
    gathered_weight = lax.all_gather(new_weight, "shard", axis=0, tiled=True)
    return (new_momentum, gathered_weight)


MESH = pl.DeviceIdType.MESH
BF16 = jnp.bfloat16
F32 = jnp.float32
X_CHIPS = 2
Y_CHIPS = 2
CORES = 2
TILES = 3
PLANES = 4
PARTS = 2


def dot_nt(left, right):
    return lax.dot_general(
        left, right, (((1,), (1,)), ((), ())), preferred_element_type=jnp.float32
    )


def dot_nn(left, right, precision=None):
    return lax.dot_general(
        left,
        right,
        (((1,), (0,)), ((), ())),
        precision=precision,
        preferred_element_type=jnp.float32,
    )


def eye(rows, cols, row_first, col_first):
    row_ids = lax.broadcasted_iota(jnp.int32, (rows, cols), 0) + row_first
    col_ids = lax.broadcasted_iota(jnp.int32, (rows, cols), 1) + col_first
    return row_ids == col_ids


def total(value):
    return jnp.sum(jnp.sum(value, axis=0, keepdims=True), axis=1, keepdims=True)


class Place:
    def __init__(self):
        self.s = lax.axis_index("shard")
        self.t = lax.axis_index("tensor")
        self.z, self.y = self.s // Y_CHIPS, self.s % Y_CHIPS
        self.x, self.c = self.t // CORES, self.t % CORES
        z, y, x, c = self.z, self.y, self.x, self.c
        self.mid = ((z + 1) // 2) % 2
        self.own = (y, x)
        self.p = (c * (1 - y) + (1 - c) * y, (1 - c) * (1 - x) + c * x)
        self.q = ((1 - c) * (1 - y) + c * y, c * (1 - x) + (1 - c) * x)
        self.d = (1 - y, 1 - x)

    def id(self, z, chip, c):
        return (z * Y_CHIPS + chip[0], chip[1] * CORES + c)

    def plane(self, k):
        z = self.z
        if isinstance(k, int):
            return [z, z + 1 - 2 * (z % 2), (z + 2) % PLANES, PLANES - 1 - z][k]
        return (k - 2) * (PLANES - 1 - z) + (3 - k) * ((z + 2) % PLANES)

    def slab(self, far, j):
        return self.plane(self.nth(j)) * Y_CHIPS + [self.y, 1 - self.y][far]

    def nth(self, j):
        return [0, 1, 2 + self.mid, 3 - self.mid][j]


class Stream:
    SLOTS = {"L": (8, 4), "P": (4, 4), "Q": (4, 4), "D": (8, 4)}

    def __init__(self, place, buf, width, first, count, sems):
        self.at, self.buf, self.width = place, buf, width
        self.first, self.count, self.sems = first, count, sems

    def block(self, k, chip, c):
        p = self.at
        rows = pl.multiple_of((c * X_CHIPS + chip[1]) * self.width + self.first, 16)
        return self.buf.at[p.plane(k) * Y_CHIPS + chip[0], pl.ds(rows, self.count), :]

    def copy(self, kind, index, ref, target, slot=None):
        send, recv = self.sems[kind]
        return pltpu.make_async_remote_copy(
            src_ref=ref,
            dst_ref=ref,
            send_sem=send.at[index if slot is None else slot],
            recv_sem=recv.at[index],
            device_id=target,
            device_id_type=MESH,
        )

    def arrive(self, kind, index, ref):
        p = self.at
        self.copy(kind, index, ref, p.id(p.z, p.own, 1 - p.c), 0).wait_recv()

    def to_p(self, kind, index, ref):
        p = self.at
        self.copy(kind, index, ref, p.id(p.z, p.p, p.c)).start()

    def to_q(self, kind, index, ref):
        p = self.at
        self.copy(kind, index, ref, p.id(p.z, p.q, p.c)).start()

    def to_plane(self, kind, index, ref, k, slot):
        p = self.at
        self.copy(kind, index, ref, p.id(p.plane(k), p.own, p.c), slot).start()

    def mid_to_plane(self, kind, index, ref, k, slot):
        @pl.when(self.at.mid == 1)
        def _():
            self.to_plane(kind, index, ref, k, slot)

    def own(self):
        p = self.at
        return self.block(0, p.own, p.c)

    def own_across(self):
        self.to_p("P", 0, self.own())
        self.to_q("Q", 0, self.own())

    def own_along(self):
        self.to_plane("L", 1, self.own(), 1, 1)
        self.mid_to_plane("L", 3, self.own(), 3, 3)

    def line(self, j):
        p = self.at
        k = p.nth(j)
        ref = self.block(k, p.own, p.c)
        self.arrive("L", k, ref)
        if j == 1:
            self.mid_to_plane("L", 2, ref, 3, 2)
        elif j == 2:
            self.mid_to_plane("L", 2, ref, 1, 6)
        else:
            self.mid_to_plane("L", 3, ref, 1, 7)
        self.to_p("P", k, ref)
        self.to_q("Q", k, ref)

    def pcol(self, j):
        p = self.at
        k = p.nth(j)
        ref = self.block(k, p.p, p.c)
        self.arrive("P", k, ref)
        if j == 3:
            self.to_q("D", k, ref)

    def qcol(self, j):
        p = self.at
        k = p.nth(j)
        ref = self.block(k, p.q, p.c)
        self.arrive("Q", k, ref)
        if j == 0:
            self.to_p("D", 0, ref)

    def diag(self, j):
        p = self.at
        k = p.nth(j)
        ref = self.block(k, p.d, p.c)
        self.arrive("D", k, ref)
        if j == 0:
            self.to_plane("D", 1, ref, 1, 5)
            self.mid_to_plane("D", 3, ref, 3, 7)
        if j == 2:
            self.mid_to_plane("D", 2, ref, 1, 6)

    def finish(self):
        p = self.at

        def sent(kind, slot):
            self.copy(kind, 0, self.own(), p.id(p.z, p.own, 1 - p.c), slot).wait_send()

        for k in range(4):
            sent("P", k)
            sent("Q", k)
        sent("L", 1)
        sent("D", 0)
        sent("D", 3 - p.mid)
        sent("D", 5)

        @pl.when(p.mid == 1)
        def _():
            for slot in (2, 3, 6, 7):
                sent("L", slot)
            for slot in (6, 7):
                sent("D", slot)


class Sibling:
    def __init__(self, place, buf, sems):
        self.at, self.buf, self.sems = place, buf, sems

    def copy(self, far, j, c):
        p = self.at
        k = p.nth(j)
        half = self.buf.shape[1] // CORES
        rows = pl.multiple_of(c * half, 16)
        ref = self.buf.at[p.slab(far, j), pl.ds(rows, half), :]
        return pltpu.make_async_remote_copy(
            src_ref=ref,
            dst_ref=ref,
            send_sem=self.sems[0].at[PLANES * far + k],
            recv_sem=self.sems[1].at[PLANES * far + k],
            device_id=p.id(p.z, p.own, 1 - p.c),
            device_id_type=MESH,
        )

    def send(self, far, j):
        self.copy(far, j, self.at.c).start()

    def arrive(self, far, j):
        self.copy(far, j, 1 - self.at.c).wait_recv()

    def finish(self):
        for far in range(2):
            for j in range(PLANES):
                self.copy(far, j, self.at.c).wait_send()


def cov_slab(buf, cov, slab, add):
    tile = cov.shape[0] // TILES
    for i in range(TILES):
        for j in range(i, TILES):
            rows, cols = pl.ds(i * tile, tile), pl.ds(j * tile, tile)
            product = dot_nt(buf[slab, rows, :], buf[slab, cols, :])
            cov[rows, cols] = cov[rows, cols] + product if add else product


def right_slab(buf, projected, right, slab, add):
    tile = right.shape[0] // TILES
    for i in range(TILES):
        rows = pl.ds(i * tile, tile)
        product = dot_nt(buf[slab, rows, :], projected[slab])
        right[rows, :] = right[rows, :] + product if add else product


def damp(cov, factor, damping):
    d = cov.shape[0]
    step = d // 9
    trace = jnp.zeros((1, 1), F32)
    for i in range(9):
        part = cov[i * step : (i + 1) * step, i * step : (i + 1) * step]
        trace = trace + total(jnp.where(eye(step, step, 0, 0), part, 0.0))
    shift = damping * trace / d

    tile = d // TILES
    unit = eye(tile, tile, 0, 0)
    ones = unit.astype(F32).astype(BF16)
    squares = jnp.zeros((1, tile), F32)
    for i in range(TILES):
        for j in range(i, TILES):
            rows, cols = slice(i * tile, (i + 1) * tile), slice(j * tile, (j + 1) * tile)
            piece = cov[rows, cols]
            if i == j:
                piece = piece + jnp.where(unit, shift, 0.0)
            low = piece.astype(BF16)
            factor[rows, cols] = low
            wide = low.astype(F32)
            square = jnp.sum(wide * wide, axis=0, keepdims=True)
            squares = squares + (square if i == j else 2.0 * square)
            if i != j:
                factor[cols, rows] = dot_nt(ones, low).astype(BF16)
    return jnp.sqrt(jnp.sum(squares, axis=1, keepdims=True))


def horner_steps(factor, work, coeffs, first, norm):
    rows, d = work.shape
    tile = d // TILES
    terms = coeffs.shape[0]

    def begin():
        start = pl.multiple_of(first, rows)
        top = jnp.full((1, 1), coeffs[terms - 1], F32).astype(BF16).astype(F32)
        diag = eye(rows, d, first, 0)
        value = jnp.where(diag, coeffs[terms - 2] + coeffs[terms - 1], 0.0)
        work[...] = value - factor[pl.ds(start, rows), :].astype(F32) * (top / norm())

    def term(index):
        low = work[...].astype(BF16)
        inv = 1.0 / norm()
        for j in range(TILES):
            cols = slice(j * tile, (j + 1) * tile)
            product = dot_nn(low, factor[:, cols])
            held = jnp.where(eye(rows, tile, first, j * tile), coeffs[index], 0.0)
            work[:, cols] = held + work[:, cols] - product * inv

    return [begin] + [functools.partial(term, k) for k in range(terms - 3, -1, -1)]


PLAN = [
    "GZ GX AZ AX",
    "GQ0m GQ0e GO2m GP0e",
    "GO1m GD0m GO3m GO1e",
    "AP0e AQ0m AQ0e GP0m",
    "GD0e AO1m GD2m GF0m",
    "GF0e GO2e AN0e GN0m",
    "AP0m GP2m GP1m GQ1m",
    "GD1e GP1e AN0m GQ2m",
    "AD0e GN1m GQ1e GF1e",
    "GF2m GN1e GO3e GQ2e",
    "AO1e GN0e GD1m GP2e",
    "GN2m an0 GF1m GP3m",
    "AO3m GQ3m gf0 AF0e",
    "gn1 GN3m GQ3e AO2m",
    "GD2e GF2e AD0m gn0",
    "GP3e gf1 AD1m AF0m",
    "gf2 AP1e GN3e GN2e",
    "AO3e AP1m AQ1m AN1m",
    "af0 AQ1e gn3 GD3m",
    "GD3e GF3e GF3m gn2",
    "AD2m AN1e AO2e gf3",
    "gd AQ3m AP3m AP3e",
    "h0 h1 h2 AN3m",
    "hl an1 AF1m AD1e",
    "AQ3e AN3e AF1e AP2e",
    "p0 p2 AQ2m AP2m",
    "p1 p3 AQ2e rn0",
    "AN2m AF2m rn1 rf0",
    "AN2e fg AD3m AD2e",
    "AF2e an3 AD3e AF3e",
    "rn3 af1 AF3m an2",
    "af2 rn2 af3 rf1",
    "rf3 rf2",
]


def step_kernel(
    acts_ref,
    grads_ref,
    weight_ref,
    momentum_ref,
    damping_ref,
    coeffs_ref,
    new_momentum_ref,
    weights_ref,
    acts_all,
    grads_all,
    cov,
    act_cov,
    factor,
    grad_work,
    grad_low,
    act_work,
    projected,
    right,
    weight_all,
    weight_own,
    momentum,
    sums,
    local_sems,
    sum_send,
    sum_recv,
    *sems,
):
    p = Place()
    s, t = p.s, p.t
    shards, tensors = Y_CHIPS * PLANES, X_CHIPS * CORES
    width = grads_ref.shape[0]
    height, d = weight_ref.shape[0], cov.shape[0]
    barrier = pltpu.get_barrier_semaphore()
    others = []
    for hop in (4, 5, 3, 2, 6, 1, 7, 0):
        for k in range(tensors):
            if hop + k > 0:
                others.append(((s + hop) % shards, (t + k) % tensors))
    greeted = [p.id(p.z, p.p, p.c), p.id(p.z, p.q, p.c), p.id(p.z, p.own, 1 - p.c)]
    greeted += [p.id(p.plane(k), p.own, p.c) for k in range(1, PLANES)]
    for other in greeted:
        pl.semaphore_signal(barrier, inc=1, device_id=other, device_id_type=MESH)

    place = p.c * X_CHIPS + p.x
    own_rows = pl.ds(pl.multiple_of(place * width, width), width)
    loads = []
    for k, (src, dst) in enumerate(
        [
            (grads_ref, grads_all.at[s, own_rows, :]),
            (acts_ref, acts_all.at[s, own_rows, :]),
            (weight_ref, weight_own),
            (momentum_ref, momentum),
        ]
    ):
        loads.append(pltpu.make_async_copy(src, dst, local_sems.at[k]))
        loads[-1].start()

    pairs = list(zip(sems[0::2], sems[1::2]))
    kinds = list(Stream.SLOTS)
    part = width // PARTS
    streams, siblings = {}, {}
    for name, buf in (("G", grads_all), ("A", acts_all)):
        streams[name] = []
        for k in range(PARTS):
            own = dict(zip(kinds, pairs[: len(kinds)]))
            pairs = pairs[len(kinds) :]
            streams[name].append(Stream(p, buf, width, k * part, part, own))
        siblings[name] = Sibling(p, buf, pairs[0])
        pairs = pairs[1:]
    line_pair, cross_pair = pairs

    loads[0].wait()
    loads[1].wait()
    pl.semaphore_wait(barrier, len(greeted))

    def relay(word):
        if word[1] in "NF":
            siblings[word[0]].send("NF".index(word[1]), int(word[2]))
            return
        for stream in streams[word[0]]:
            if word[1] in "XZ":
                {"X": stream.own_across, "Z": stream.own_along}[word[1]]()
            else:
                move = {"O": stream.line, "P": stream.pcol, "Q": stream.qcol, "D": stream.diag}[word[1]]
                move(int(word[2]))

    def settle(name):
        siblings[name].finish()
        for stream in streams[name]:
            stream.finish()

    norms = {}
    horner_g = horner_steps(factor, grad_work, coeffs_ref, place * width, lambda: norms["g"])
    started = set()

    def compute(word):
        kind = word[0]
        if word == "fg":
            settle("G")
        elif word == "gd":
            norms["g"] = damp(cov, factor, damping_ref[1])
        elif word == "hl":
            grad_low[...] = grad_work[...].astype(BF16)
        elif kind == "h":
            horner_g[int(word[1])]()
        elif kind == "p":
            for k in (2 * int(word[1]), 2 * int(word[1]) + 1):
                projected[k] = dot_nn(grad_low[...], grads_all[k]).astype(BF16)
        else:
            far, j = "nf".index(word[1]), int(word[2])
            slab = p.slab(far, j)
            add = kind in started
            started.add(kind)
            if kind == "r":
                right_slab(acts_all, projected, right, slab, add)
            else:
                name = kind.upper()
                siblings[name].arrive(far, j)
                buf, out = {"G": (grads_all, cov), "A": (acts_all, act_cov)}[name]
                cov_slab(buf, out, slab, add)

    def group_of(word):
        if word[0] not in "GA":
            return word
        return word[-1] if word[-1] in "em" else "all"

    for group, words in itertools.groupby(" ".join(PLAN).split(), group_of):
        if group == "all":
            for word in words:
                relay(word)
        elif group in ("e", "m"):

            @pl.when(p.mid == "em".index(group))
            def _():
                for word in words:
                    relay(word[:-1])
        else:
            compute(group)

    act_norm = damp(act_cov, factor, damping_ref[0])
    block, inner = s * height // width, s * height % width
    first = (block % CORES * X_CHIPS + block // CORES) * width + inner
    for run in horner_steps(factor, act_work, coeffs_ref, first, lambda: act_norm):
        run()
    update = dot_nn(act_work[...], right[...], lax.Precision.HIGHEST)

    me = s * tensors + t
    sums[me] = jnp.broadcast_to(total(update * update), sums.shape[1:])
    count = shards * tensors
    for k, other in enumerate(others):
        pltpu.make_async_remote_copy(
            src_ref=sums.at[me],
            dst_ref=sums.at[me],
            send_sem=sum_send,
            recv_sem=sum_recv,
            device_id=other,
            device_id_type=MESH,
        ).start()
    loads[2].wait()
    loads[3].wait()
    settle("A")
    everyone = pltpu.make_async_remote_copy(
        src_ref=sums.at[: count - 1],
        dst_ref=sums.at[: count - 1],
        send_sem=sum_send,
        recv_sem=sum_recv,
        device_id=others[0],
        device_id_type=MESH,
    )
    everyone.wait_recv()
    square_sum = jnp.sum(sums[...], axis=0)[:, 0:1]
    mean_square = square_sum / (d * d)
    new = 0.9 * momentum[...] + update / jnp.sqrt(mean_square + 1e-06)
    low = (weight_own[...].astype(F32) - 0.1 * new).astype(BF16)
    main = weight_all.shape[2]
    rest = width - main
    weight_all[s, :height, :] = low[:, :main]

    cuts = [slice(0, 96), slice(96, weight_all.shape[1])]

    def push(slab, pair, k, cut, target, into=weight_all):
        copy = pltpu.make_async_remote_copy(
            src_ref=weight_all.at[slab, cuts[cut], :],
            dst_ref=into.at[slab, cuts[cut], :],
            send_sem=pair[0].at[k, cut],
            recv_sem=pair[1].at[k, cut],
            device_id=target,
            device_id_type=MESH,
        )
        copy.start()
        return copy

    across = (p.z * Y_CHIPS + 1 - p.y, t)
    order = [p.nth(j) for j in range(PLANES - 1, 0, -1)]
    crossed, lines = [], []
    for cut in range(len(cuts)):
        if cut == 1:
            ones = eye(rest, rest, 0, 0).astype(F32).astype(BF16)
            weight_all[s, height:, :height] = dot_nt(ones, low[:, main:]).astype(BF16)
        crossed.append(push(s, cross_pair, 0, cut, across, weights_ref))
        for k in order:
            lines.append((k, cut, push(s, line_pair, k, cut, (p.plane(k) * Y_CHIPS + p.y, t))))
    momentum[...] = new
    stores = [pltpu.make_async_copy(momentum, new_momentum_ref, local_sems.at[4])]
    stores[0].start()

    def keep(slab):
        stores.append(
            pltpu.make_async_copy(
                weight_all.at[slab], weights_ref.at[slab], local_sems.at[4 + len(stores)]
            )
        )
        stores[-1].start()

    keep(s)
    for k in order:
        slab = p.plane(k) * Y_CHIPS + p.y
        for j, cut, copy in lines:
            if j is k:
                copy.wait_recv()
                crossed.append(push(slab, cross_pair, k, cut, across, weights_ref))
        keep(slab)
    everyone.wait_send()
    for _, _, copy in lines:
        copy.wait_send()
    for copy in stores:
        copy.wait()
    for copy in crossed:
        copy.wait()


def finish_kernel(momentum_ref, weights_ref, new_momentum_ref, gathered_ref):
    shards, rows, main = weights_ref.shape
    width = gathered_ref.shape[0]
    height = rows - (width - main)
    new_momentum_ref[...] = momentum_ref[...]
    low = jnp.concatenate([weights_ref[k, :height, :] for k in range(shards)], axis=0)
    ones = eye(main, main, 0, 0).astype(F32).astype(BF16)
    gathered_ref[:main, :] = dot_nt(ones, low).astype(BF16)
    for k in range(shards):
        gathered_ref[main:, k * height : (k + 1) * height] = weights_ref[k, height:, :height]


def on_device_whole(acts, outgrads, weight, momentum, damping, coeffs):
    tokens, width = acts.shape
    height = weight.shape[0]
    shards, tensors = Y_CHIPS * PLANES, X_CHIPS * CORES
    d = width * tensors
    main = width // 128 * 128
    packed = (shards, height + width - main, main)
    vmem = pl.BlockSpec(memory_space=pltpu.VMEM)
    smem = pl.BlockSpec(memory_space=pltpu.SMEM)
    anywhere = pl.BlockSpec(memory_space=pl.ANY)
    dma = pltpu.SemaphoreType.DMA
    sems = []
    for _ in range(2):
        for pair in list(Stream.SLOTS.values()) * PARTS + [(CORES * PLANES, CORES * PLANES)]:
            sems += [dma((count,)) for count in pair]
    new_momentum, weights = pl.pallas_call(
        step_kernel,
        out_shape=(
            jax.ShapeDtypeStruct((height, width), F32),
            jax.ShapeDtypeStruct(packed, BF16),
        ),
        in_specs=[anywhere] * 4 + [smem] * 2,
        out_specs=(anywhere, anywhere),
        scratch_shapes=[
            pltpu.VMEM((shards, d, tokens), BF16),
            pltpu.VMEM((shards, d, tokens), BF16),
            pltpu.VMEM((d, d), F32),
            pltpu.VMEM((d, d), F32),
            pltpu.VMEM((d, d), BF16),
            pltpu.VMEM((width, d), F32),
            pltpu.VMEM((width, d), BF16),
            pltpu.VMEM((height, d), F32),
            pltpu.VMEM((shards, width, tokens), BF16),
            pltpu.VMEM((d, width), F32),
            pltpu.VMEM(packed, BF16),
            pltpu.VMEM((height, width), BF16),
            pltpu.VMEM((height, width), F32),
            pltpu.VMEM((shards * tensors, 1, 128), F32),
            dma((5 + PLANES,)),
            dma,
            dma,
        ]
        + sems
        + [dma((PLANES, 2))] * 4,
        compiler_params=pltpu.CompilerParams(
            collective_id=0, has_side_effects=True, vmem_limit_bytes=62 * 2**20
        ),
    )(acts.T, outgrads.T, weight, momentum, damping, coeffs)
    new_momentum, gathered = pl.pallas_call(
        finish_kernel,
        out_shape=(
            jax.ShapeDtypeStruct((height, width), F32),
            jax.ShapeDtypeStruct((width, d), BF16),
        ),
        in_specs=[vmem, vmem],
        out_specs=(vmem, vmem),
    )(new_momentum, weights)
    return new_momentum, gathered.T


def solution(mesh):
    in_specs = (
        P("shard", "tensor"),
        P("shard", "tensor"),
        P("shard", "tensor"),
        P("shard", "tensor"),
        P(),
        P(),
    )
    out_specs = (P("shard", "tensor"), P(None, "tensor"))
    shape = (mesh.shape["shard"], mesh.shape["tensor"])
    whole = shape == (Y_CHIPS * PLANES, X_CHIPS * CORES)

    def local(acts, *rest):
        held = 2 * acts.dtype.itemsize * acts.size * shape[0] * shape[1]
        if whole and held <= 24 * 2**20:
            return on_device_whole(acts, *rest)
        return on_device(acts, *rest)

    return jax.shard_map(
        local, mesh=mesh, in_specs=in_specs, out_specs=out_specs, check_vma=False
    )
```

```python
import functools
import itertools

import jax
import jax.numpy as jnp
from jax import lax
from jax.experimental import pallas as pl
from jax.experimental.pallas import tpu as pltpu
from jax.sharding import PartitionSpec as P

D = 1152


def horner_columns(factor, coeffs, first_col, col_count, bound_norm):
    extent = factor.shape[0]
    row_ids = lax.broadcasted_iota(jnp.int32, (extent, col_count), 0)
    col_ids = lax.broadcasted_iota(jnp.int32, (extent, col_count), 1) + first_col
    identity_cols = (row_ids == col_ids).astype(jnp.float32)
    term_count = coeffs.shape[0]
    iterate = coeffs[term_count - 1] * identity_cols
    for term_index in range(term_count - 2, -1, -1):
        product = jnp.dot(factor, iterate.astype(jnp.bfloat16), preferred_element_type=jnp.float32)
        iterate = coeffs[term_index] * identity_cols + iterate - product / bound_norm
    return iterate


def tokens_product(left, right):
    return lax.dot_general(
        left, right, (((0,), (0,)), ((), ())), preferred_element_type=jnp.float32
    )


def on_device(acts, outgrads, weight, momentum, damping, coeffs):
    row_count = weight.shape[0]
    col_count = weight.shape[1]
    row_first = lax.axis_index("shard") * row_count
    col_first = lax.axis_index("tensor") * col_count
    full_acts, full_grads = (
        lax.all_gather(acts, "tensor", axis=1, tiled=True),
        lax.all_gather(outgrads, "tensor", axis=1, tiled=True),
    )
    local_squares = jnp.stack(
        [
            jnp.sum(jnp.square(acts.astype(jnp.float32))),
            jnp.sum(jnp.square(outgrads.astype(jnp.float32))),
        ]
    )
    traces = lax.psum(local_squares, ("shard", "tensor"))
    act_part = tokens_product(full_acts, acts)
    grad_part = tokens_product(full_grads, outgrads)
    stats = lax.psum_scatter(
        jnp.concatenate([act_part, grad_part], axis=1), "shard", scatter_dimension=0, tiled=True
    )
    row_ids = lax.broadcasted_iota(jnp.int32, (row_count, col_count), 0) + row_first
    col_ids = lax.broadcasted_iota(jnp.int32, (row_count, col_count), 1) + col_first
    diag_mask = (row_ids == col_ids).astype(jnp.float32)
    act_piece = (stats[:, :col_count] + damping[0] * traces[0] / D * diag_mask).astype(jnp.bfloat16)
    grad_piece = (stats[:, col_count:] + damping[1] * traces[1] / D * diag_mask).astype(
        jnp.bfloat16
    )
    act_wide, grad_wide = (
        lax.all_gather(act_piece, "tensor", axis=1, tiled=True),
        lax.all_gather(grad_piece, "tensor", axis=1, tiled=True),
    )
    act_full, grad_full = (
        lax.all_gather(act_wide, "shard", axis=0, tiled=True),
        lax.all_gather(grad_wide, "shard", axis=0, tiled=True),
    )
    act_scale = jnp.sqrt(jnp.sum(jnp.square(act_full.astype(jnp.float32))))
    grad_scale = jnp.sqrt(jnp.sum(jnp.square(grad_full.astype(jnp.float32))))
    act_inverse = horner_columns(act_full, coeffs, row_first, row_count, act_scale)
    grad_inverse = horner_columns(grad_full, coeffs, col_first, col_count, grad_scale).astype(
        jnp.bfloat16
    )
    projected = jnp.dot(full_grads, grad_inverse, preferred_element_type=jnp.float32).astype(
        jnp.bfloat16
    )
    right_term = tokens_product(full_acts, projected)
    right_product = lax.psum(right_term, "shard")
    update = lax.dot_general(
        act_inverse,
        right_product,
        (((0,), (0,)), ((), ())),
        precision=lax.Precision.HIGHEST,
        preferred_element_type=jnp.float32,
    )
    square_sum = lax.psum(jnp.sum(update * update), ("shard", "tensor"))
    mean_square = square_sum / (D * D)
    new_momentum = 0.9 * momentum + update / jnp.sqrt(mean_square + 1e-06)
    new_weight = (weight.astype(jnp.float32) - 0.1 * new_momentum).astype(jnp.bfloat16)
    gathered_weight = lax.all_gather(new_weight, "shard", axis=0, tiled=True)
    return (new_momentum, gathered_weight)


MESH = pl.DeviceIdType.MESH
BF16 = jnp.bfloat16
F32 = jnp.float32
X_CHIPS = 2
Y_CHIPS = 2
CORES = 2
TILES = 3
PLANES = 4
PARTS = 2


def dot_nt(left, right):
    return lax.dot_general(
        left, right, (((1,), (1,)), ((), ())), preferred_element_type=jnp.float32
    )


def dot_nn(left, right, precision=None):
    return lax.dot_general(
        left,
        right,
        (((1,), (0,)), ((), ())),
        precision=precision,
        preferred_element_type=jnp.float32,
    )


def eye(rows, cols, row_first, col_first):
    row_ids = lax.broadcasted_iota(jnp.int32, (rows, cols), 0) + row_first
    col_ids = lax.broadcasted_iota(jnp.int32, (rows, cols), 1) + col_first
    return row_ids == col_ids


def total(value):
    return jnp.sum(jnp.sum(value, axis=0, keepdims=True), axis=1, keepdims=True)


class Place:
    def __init__(self):
        self.s = lax.axis_index("shard")
        self.t = lax.axis_index("tensor")
        self.z, self.y = self.s // Y_CHIPS, self.s % Y_CHIPS
        self.x, self.c = self.t // CORES, self.t % CORES
        z, y, x, c = self.z, self.y, self.x, self.c
        self.mid = ((z + 1) // 2) % 2
        self.own = (y, x)
        self.p = (c * (1 - y) + (1 - c) * y, (1 - c) * (1 - x) + c * x)
        self.q = ((1 - c) * (1 - y) + c * y, c * (1 - x) + (1 - c) * x)
        self.d = (1 - y, 1 - x)

    def id(self, z, chip, c):
        return (z * Y_CHIPS + chip[0], chip[1] * CORES + c)

    def plane(self, k):
        z = self.z
        if isinstance(k, int):
            return [z, z + 1 - 2 * (z % 2), (z + 2) % PLANES, PLANES - 1 - z][k]
        return (k - 2) * (PLANES - 1 - z) + (3 - k) * ((z + 2) % PLANES)

    def slab(self, far, j):
        return self.plane(self.nth(j)) * Y_CHIPS + [self.y, 1 - self.y][far]

    def nth(self, j):
        return [0, 1, 2 + self.mid, 3 - self.mid][j]


class Stream:
    SLOTS = {"L": (8, 4), "P": (4, 4), "Q": (4, 4), "D": (8, 4)}

    def __init__(self, place, buf, width, first, count, sems):
        self.at, self.buf, self.width = place, buf, width
        self.first, self.count, self.sems = first, count, sems

    def block(self, k, chip, c):
        p = self.at
        rows = pl.multiple_of((c * X_CHIPS + chip[1]) * self.width + self.first, 16)
        return self.buf.at[p.plane(k) * Y_CHIPS + chip[0], pl.ds(rows, self.count), :]

    def copy(self, kind, index, ref, target, slot=None):
        send, recv = self.sems[kind]
        return pltpu.make_async_remote_copy(
            src_ref=ref,
            dst_ref=ref,
            send_sem=send.at[index if slot is None else slot],
            recv_sem=recv.at[index],
            device_id=target,
            device_id_type=MESH,
        )

    def arrive(self, kind, index, ref):
        p = self.at
        self.copy(kind, index, ref, p.id(p.z, p.own, 1 - p.c), 0).wait_recv()

    def to_p(self, kind, index, ref):
        p = self.at
        self.copy(kind, index, ref, p.id(p.z, p.p, p.c)).start()

    def to_q(self, kind, index, ref):
        p = self.at
        self.copy(kind, index, ref, p.id(p.z, p.q, p.c)).start()

    def to_plane(self, kind, index, ref, k, slot):
        p = self.at
        self.copy(kind, index, ref, p.id(p.plane(k), p.own, p.c), slot).start()

    def mid_to_plane(self, kind, index, ref, k, slot):
        @pl.when(self.at.mid == 1)
        def _():
            self.to_plane(kind, index, ref, k, slot)

    def own(self):
        p = self.at
        return self.block(0, p.own, p.c)

    def own_across(self):
        self.to_p("P", 0, self.own())
        self.to_q("Q", 0, self.own())

    def own_along(self):
        self.to_plane("L", 1, self.own(), 1, 1)
        self.mid_to_plane("L", 3, self.own(), 3, 3)

    def line(self, j):
        p = self.at
        k = p.nth(j)
        ref = self.block(k, p.own, p.c)
        self.arrive("L", k, ref)
        if j == 1:
            self.mid_to_plane("L", 2, ref, 3, 2)
        elif j == 2:
            self.mid_to_plane("L", 2, ref, 1, 6)
        else:
            self.mid_to_plane("L", 3, ref, 1, 7)
        self.to_p("P", k, ref)
        self.to_q("Q", k, ref)

    def pcol(self, j):
        p = self.at
        k = p.nth(j)
        ref = self.block(k, p.p, p.c)
        self.arrive("P", k, ref)
        if j == 3:
            self.to_q("D", k, ref)

    def qcol(self, j):
        p = self.at
        k = p.nth(j)
        ref = self.block(k, p.q, p.c)
        self.arrive("Q", k, ref)
        if j == 0:
            self.to_p("D", 0, ref)

    def diag(self, j):
        p = self.at
        k = p.nth(j)
        ref = self.block(k, p.d, p.c)
        self.arrive("D", k, ref)
        if j == 0:
            self.to_plane("D", 1, ref, 1, 5)
            self.mid_to_plane("D", 3, ref, 3, 7)
        if j == 2:
            self.mid_to_plane("D", 2, ref, 1, 6)

    def finish(self):
        p = self.at

        def sent(kind, slot):
            self.copy(kind, 0, self.own(), p.id(p.z, p.own, 1 - p.c), slot).wait_send()

        for k in range(4):
            sent("P", k)
            sent("Q", k)
        sent("L", 1)
        sent("D", 0)
        sent("D", 3 - p.mid)
        sent("D", 5)

        @pl.when(p.mid == 1)
        def _():
            for slot in (2, 3, 6, 7):
                sent("L", slot)
            for slot in (6, 7):
                sent("D", slot)


class Sibling:
    def __init__(self, place, buf, sems):
        self.at, self.buf, self.sems = place, buf, sems

    def copy(self, far, j, c):
        p = self.at
        k = p.nth(j)
        half = self.buf.shape[1] // CORES
        rows = pl.multiple_of(c * half, 16)
        ref = self.buf.at[p.slab(far, j), pl.ds(rows, half), :]
        return pltpu.make_async_remote_copy(
            src_ref=ref,
            dst_ref=ref,
            send_sem=self.sems[0].at[PLANES * far + k],
            recv_sem=self.sems[1].at[PLANES * far + k],
            device_id=p.id(p.z, p.own, 1 - p.c),
            device_id_type=MESH,
        )

    def send(self, far, j):
        self.copy(far, j, self.at.c).start()

    def arrive(self, far, j):
        self.copy(far, j, 1 - self.at.c).wait_recv()

    def finish(self):
        for far in range(2):
            for j in range(PLANES):
                self.copy(far, j, self.at.c).wait_send()


def cov_slab(buf, cov, slab, add):
    tile = cov.shape[0] // TILES
    for i in range(TILES):
        for j in range(i, TILES):
            rows, cols = pl.ds(i * tile, tile), pl.ds(j * tile, tile)
            product = dot_nt(buf[slab, rows, :], buf[slab, cols, :])
            cov[rows, cols] = cov[rows, cols] + product if add else product


def right_slab(buf, projected, right, slab, add):
    tile = right.shape[0] // TILES
    for i in range(TILES):
        rows = pl.ds(i * tile, tile)
        product = dot_nt(buf[slab, rows, :], projected[slab])
        right[rows, :] = right[rows, :] + product if add else product


def damp(cov, factor, damping):
    d = cov.shape[0]
    step = d // 9
    trace = jnp.zeros((1, 1), F32)
    for i in range(9):
        part = cov[i * step : (i + 1) * step, i * step : (i + 1) * step]
        trace = trace + total(jnp.where(eye(step, step, 0, 0), part, 0.0))
    shift = damping * trace / d

    tile = d // TILES
    unit = eye(tile, tile, 0, 0)
    ones = unit.astype(F32).astype(BF16)
    squares = jnp.zeros((1, tile), F32)
    for i in range(TILES):
        for j in range(i, TILES):
            rows, cols = slice(i * tile, (i + 1) * tile), slice(j * tile, (j + 1) * tile)
            piece = cov[rows, cols]
            if i == j:
                piece = piece + jnp.where(unit, shift, 0.0)
            low = piece.astype(BF16)
            factor[rows, cols] = low
            wide = low.astype(F32)
            square = jnp.sum(wide * wide, axis=0, keepdims=True)
            squares = squares + (square if i == j else 2.0 * square)
            if i != j:
                factor[cols, rows] = dot_nt(ones, low).astype(BF16)
    return jnp.sqrt(jnp.sum(squares, axis=1, keepdims=True))


def horner_steps(factor, work, coeffs, first, norm):
    rows, d = work.shape
    tile = d // TILES
    terms = coeffs.shape[0]

    def begin():
        start = pl.multiple_of(first, rows)
        top = jnp.full((1, 1), coeffs[terms - 1], F32).astype(BF16).astype(F32)
        diag = eye(rows, d, first, 0)
        value = jnp.where(diag, coeffs[terms - 2] + coeffs[terms - 1], 0.0)
        work[...] = value - factor[pl.ds(start, rows), :].astype(F32) * (top / norm())

    def term(index):
        low = work[...].astype(BF16)
        inv = 1.0 / norm()
        for j in range(TILES):
            cols = slice(j * tile, (j + 1) * tile)
            product = dot_nn(low, factor[:, cols])
            held = jnp.where(eye(rows, tile, first, j * tile), coeffs[index], 0.0)
            work[:, cols] = held + work[:, cols] - product * inv

    return [begin] + [functools.partial(term, k) for k in range(terms - 3, -1, -1)]


PLAN = [
    "GZ GX AZ AX",
    "GQ0m GQ0e GO2m GP0e",
    "GO1m GD0m GO3m GO1e",
    "AP0e AQ0m AQ0e GP0m",
    "GD0e AO1m GD2m GF0m",
    "GF0e GO2e AN0e GN0m",
    "AP0m GP2m GP1m GQ1m",
    "GD1e GP1e AN0m GQ2m",
    "AD0e GN1m GQ1e GF1e",
    "GF2m GN1e GO3e GQ2e",
    "AO1e GN0e GD1m GP2e",
    "GN2m an0 GF1m GP3m",
    "AO3m GQ3m gf0 AF0e",
    "gn1 GN3m GQ3e AO2m",
    "GD2e GF2e AD0m gn0",
    "GP3e gf1 AD1m AF0m",
    "gf2 AP1e GN3e GN2e",
    "AO3e AP1m AQ1m AN1m",
    "af0 AQ1e gn3 GD3m",
    "GD3e GF3e GF3m gn2",
    "AD2m AN1e AO2e gf3",
    "gd AQ3m AP3m AP3e",
    "h0 h1 h2 AN3m",
    "hl an1 AF1m AD1e",
    "AQ3e AN3e AF1e AP2e",
    "p0 p2 AQ2m AP2m",
    "p1 p3 AQ2e rn0",
    "AN2m AF2m rn1 rf0",
    "AN2e fg AD3m AD2e",
    "AF2e an3 AD3e AF3e",
    "rn3 af1 AF3m an2",
    "af2 rn2 af3 rf1",
    "rf3 rf2",
]


def step_kernel(
    acts_ref,
    grads_ref,
    weight_ref,
    momentum_ref,
    damping_ref,
    coeffs_ref,
    new_momentum_ref,
    weights_ref,
    acts_all,
    grads_all,
    cov,
    act_cov,
    factor,
    grad_work,
    grad_low,
    act_work,
    projected,
    right,
    weight_all,
    weight_own,
    momentum,
    sums,
    local_sems,
    sum_send,
    sum_recv,
    *sems,
):
    p = Place()
    s, t = p.s, p.t
    shards, tensors = Y_CHIPS * PLANES, X_CHIPS * CORES
    width = grads_ref.shape[0]
    height, d = weight_ref.shape[0], cov.shape[0]
    barrier = pltpu.get_barrier_semaphore()
    others = []
    for hop in (4, 5, 3, 2, 6, 1, 7, 0):
        for k in range(tensors):
            if hop + k > 0:
                others.append(((s + hop) % shards, (t + k) % tensors))
    place = p.c * X_CHIPS + p.x
    own_rows = pl.ds(pl.multiple_of(place * width, width), width)
    greeted = [p.id(p.z, p.p, p.c), p.id(p.z, p.q, p.c), p.id(p.z, p.own, 1 - p.c)]
    greeted += [p.id(p.plane(k), p.own, p.c) for k in range(1, PLANES)]
    loads = []
    for k, (src, dst) in enumerate(
        [
            (grads_ref, grads_all.at[s, own_rows, :]),
            (acts_ref, acts_all.at[s, own_rows, :]),
            (weight_ref, weight_own),
            (momentum_ref, momentum),
        ]
    ):
        loads.append(pltpu.make_async_copy(src, dst, local_sems.at[k]))
        loads[-1].start()
        if k == 0:
            for other in greeted:
                pl.semaphore_signal(barrier, inc=1, device_id=other, device_id_type=MESH)

    pairs = list(zip(sems[0::2], sems[1::2]))
    kinds = list(Stream.SLOTS)
    part = width // PARTS
    streams, siblings = {}, {}
    for name, buf in (("G", grads_all), ("A", acts_all)):
        streams[name] = []
        for k in range(PARTS):
            own = dict(zip(kinds, pairs[: len(kinds)]))
            pairs = pairs[len(kinds) :]
            streams[name].append(Stream(p, buf, width, k * part, part, own))
        siblings[name] = Sibling(p, buf, pairs[0])
        pairs = pairs[1:]
    line_pair, cross_pair = pairs

    loads[0].wait()
    loads[1].wait()
    pl.semaphore_wait(barrier, len(greeted))

    def relay(word):
        if word[1] in "NF":
            siblings[word[0]].send("NF".index(word[1]), int(word[2]))
            return
        for stream in streams[word[0]]:
            if word[1] in "XZ":
                {"X": stream.own_across, "Z": stream.own_along}[word[1]]()
            else:
                move = {"O": stream.line, "P": stream.pcol, "Q": stream.qcol, "D": stream.diag}[word[1]]
                move(int(word[2]))

    def settle(name):
        siblings[name].finish()
        for stream in streams[name]:
            stream.finish()

    norms = {}
    horner_g = horner_steps(factor, grad_work, coeffs_ref, place * width, lambda: norms["g"])
    started = set()

    def compute(word):
        kind = word[0]
        if word == "fg":
            settle("G")
        elif word == "gd":
            norms["g"] = damp(cov, factor, damping_ref[1])
        elif word == "hl":
            grad_low[...] = grad_work[...].astype(BF16)
        elif kind == "h":
            horner_g[int(word[1])]()
        elif kind == "p":
            for k in (2 * int(word[1]), 2 * int(word[1]) + 1):
                projected[k] = dot_nn(grad_low[...], grads_all[k]).astype(BF16)
        else:
            far, j = "nf".index(word[1]), int(word[2])
            slab = p.slab(far, j)
            add = kind in started
            started.add(kind)
            if kind == "r":
                right_slab(acts_all, projected, right, slab, add)
            else:
                name = kind.upper()
                siblings[name].arrive(far, j)
                buf, out = {"G": (grads_all, cov), "A": (acts_all, act_cov)}[name]
                cov_slab(buf, out, slab, add)

    def group_of(word):
        if word[0] not in "GA":
            return word
        return word[-1] if word[-1] in "em" else "all"

    for group, words in itertools.groupby(" ".join(PLAN).split(), group_of):
        if group == "all":
            for word in words:
                relay(word)
        elif group in ("e", "m"):

            @pl.when(p.mid == "em".index(group))
            def _():
                for word in words:
                    relay(word[:-1])
        else:
            compute(group)

    act_norm = damp(act_cov, factor, damping_ref[0])
    block, inner = s * height // width, s * height % width
    first = (block % CORES * X_CHIPS + block // CORES) * width + inner
    for run in horner_steps(factor, act_work, coeffs_ref, first, lambda: act_norm):
        run()
    update = dot_nn(act_work[...], right[...], lax.Precision.HIGHEST)

    me = s * tensors + t
    sums[me] = jnp.broadcast_to(total(update * update), sums.shape[1:])
    count = shards * tensors
    for k, other in enumerate(others):
        pltpu.make_async_remote_copy(
            src_ref=sums.at[me],
            dst_ref=sums.at[me],
            send_sem=sum_send,
            recv_sem=sum_recv,
            device_id=other,
            device_id_type=MESH,
        ).start()
    loads[2].wait()
    loads[3].wait()
    settle("A")
    everyone = pltpu.make_async_remote_copy(
        src_ref=sums.at[: count - 1],
        dst_ref=sums.at[: count - 1],
        send_sem=sum_send,
        recv_sem=sum_recv,
        device_id=others[0],
        device_id_type=MESH,
    )
    everyone.wait_recv()
    square_sum = jnp.sum(sums[...], axis=0)[:, 0:1]
    mean_square = square_sum / (d * d)
    new = 0.9 * momentum[...] + update / jnp.sqrt(mean_square + 1e-06)
    low = (weight_own[...].astype(F32) - 0.1 * new).astype(BF16)
    main = weight_all.shape[2]
    rest = width - main
    weight_all[s, :height, :] = low[:, :main]

    cuts = [slice(0, 96), slice(96, weight_all.shape[1])]

    def push(slab, pair, k, cut, target, into=weight_all):
        copy = pltpu.make_async_remote_copy(
            src_ref=weight_all.at[slab, cuts[cut], :],
            dst_ref=into.at[slab, cuts[cut], :],
            send_sem=pair[0].at[k, cut],
            recv_sem=pair[1].at[k, cut],
            device_id=target,
            device_id_type=MESH,
        )
        copy.start()
        return copy

    across = (p.z * Y_CHIPS + 1 - p.y, t)
    order = [p.nth(j) for j in range(PLANES - 1, 0, -1)]
    crossed, lines = [], []
    for cut in range(len(cuts)):
        if cut == 1:
            ones = eye(rest, rest, 0, 0).astype(F32).astype(BF16)
            weight_all[s, height:, :height] = dot_nt(ones, low[:, main:]).astype(BF16)
        crossed.append(push(s, cross_pair, 0, cut, across, weights_ref))
        for k in order:
            lines.append((k, cut, push(s, line_pair, k, cut, (p.plane(k) * Y_CHIPS + p.y, t))))
    momentum[...] = new
    stores = [pltpu.make_async_copy(momentum, new_momentum_ref, local_sems.at[4])]
    stores[0].start()

    def keep(slab):
        stores.append(
            pltpu.make_async_copy(
                weight_all.at[slab], weights_ref.at[slab], local_sems.at[4 + len(stores)]
            )
        )
        stores[-1].start()

    keep(s)
    for k in order:
        slab = p.plane(k) * Y_CHIPS + p.y
        for j, cut, copy in lines:
            if j is k:
                copy.wait_recv()
                crossed.append(push(slab, cross_pair, k, cut, across, weights_ref))
        keep(slab)
    everyone.wait_send()
    for _, _, copy in lines:
        copy.wait_send()
    for copy in stores:
        copy.wait()
    for copy in crossed:
        copy.wait()


def finish_kernel(momentum_ref, weights_ref, new_momentum_ref, gathered_ref):
    shards, rows, main = weights_ref.shape
    width = gathered_ref.shape[0]
    height = rows - (width - main)
    new_momentum_ref[...] = momentum_ref[...]
    low = jnp.concatenate([weights_ref[k, :height, :] for k in range(shards)], axis=0)
    ones = eye(main, main, 0, 0).astype(F32).astype(BF16)
    gathered_ref[:main, :] = dot_nt(ones, low).astype(BF16)
    for k in range(shards):
        gathered_ref[main:, k * height : (k + 1) * height] = weights_ref[k, height:, :height]


def on_device_whole(acts, outgrads, weight, momentum, damping, coeffs):
    tokens, width = acts.shape
    height = weight.shape[0]
    shards, tensors = Y_CHIPS * PLANES, X_CHIPS * CORES
    d = width * tensors
    main = width // 128 * 128
    packed = (shards, height + width - main, main)
    vmem = pl.BlockSpec(memory_space=pltpu.VMEM)
    smem = pl.BlockSpec(memory_space=pltpu.SMEM)
    anywhere = pl.BlockSpec(memory_space=pl.ANY)
    dma = pltpu.SemaphoreType.DMA
    sems = []
    for _ in range(2):
        for pair in list(Stream.SLOTS.values()) * PARTS + [(CORES * PLANES, CORES * PLANES)]:
            sems += [dma((count,)) for count in pair]
    new_momentum, weights = pl.pallas_call(
        step_kernel,
        out_shape=(
            jax.ShapeDtypeStruct((height, width), F32),
            jax.ShapeDtypeStruct(packed, BF16),
        ),
        in_specs=[anywhere] * 4 + [smem] * 2,
        out_specs=(anywhere, anywhere),
        scratch_shapes=[
            pltpu.VMEM((shards, d, tokens), BF16),
            pltpu.VMEM((shards, d, tokens), BF16),
            pltpu.VMEM((d, d), F32),
            pltpu.VMEM((d, d), F32),
            pltpu.VMEM((d, d), BF16),
            pltpu.VMEM((width, d), F32),
            pltpu.VMEM((width, d), BF16),
            pltpu.VMEM((height, d), F32),
            pltpu.VMEM((shards, width, tokens), BF16),
            pltpu.VMEM((d, width), F32),
            pltpu.VMEM(packed, BF16),
            pltpu.VMEM((height, width), BF16),
            pltpu.VMEM((height, width), F32),
            pltpu.VMEM((shards * tensors, 1, 128), F32),
            dma((5 + PLANES,)),
            dma,
            dma,
        ]
        + sems
        + [dma((PLANES, 2))] * 4,
        compiler_params=pltpu.CompilerParams(
            collective_id=0, has_side_effects=True, vmem_limit_bytes=62 * 2**20
        ),
    )(acts.T, outgrads.T, weight, momentum, damping, coeffs)
    new_momentum, gathered = pl.pallas_call(
        finish_kernel,
        out_shape=(
            jax.ShapeDtypeStruct((height, width), F32),
            jax.ShapeDtypeStruct((width, d), BF16),
        ),
        in_specs=[vmem, vmem],
        out_specs=(vmem, vmem),
    )(new_momentum, weights)
    return new_momentum, gathered.T


def solution(mesh):
    in_specs = (
        P("shard", "tensor"),
        P("shard", "tensor"),
        P("shard", "tensor"),
        P("shard", "tensor"),
        P(),
        P(),
    )
    out_specs = (P("shard", "tensor"), P(None, "tensor"))
    shape = (mesh.shape["shard"], mesh.shape["tensor"])
    whole = shape == (Y_CHIPS * PLANES, X_CHIPS * CORES)

    def local(acts, *rest):
        held = 2 * acts.dtype.itemsize * acts.size * shape[0] * shape[1]
        if whole and held <= 24 * 2**20:
            return on_device_whole(acts, *rest)
        return on_device(acts, *rest)

    return jax.shard_map(
        local, mesh=mesh, in_specs=in_specs, out_specs=out_specs, check_vma=False
    )
```
